512 devices in a mesh: seq: 32 (over x, z), head: 16 (over y, core).
Axes of the slice: x: 4, y: 8, z: 8, core: 2. Of those that a mesh axis runs over, the one named last changes fastest.
Arguments:
- inputs: bfloat16 [32768, 8192], P('seq', 'head'), may hold values from -6 to 6
- in_map: bfloat16 [32768, 128], P('seq'), may hold values from -1.25 to 1.25
- out_map: bfloat16 [32768, 128], P('seq'), may hold values from -1.25 to 1.25
- log_decay: float32 [64, 32768], P('head', 'seq'), may hold values from -0.8 to 0, as said below
- cotangent: bfloat16 [32768, 8192], P('seq', 'head'), may hold values from -0.4375 to 0.4375
Outputs:
- grad_inputs: float32 [32768, 8192], P('seq', 'head')
- grad_in_map: float32 [32768, 128], P(('seq', 'head'))
- grad_out_map: float32 [32768, 128], P(('seq', 'head'))
- grad_decay: float32 [64, 32768], P('head', 'seq')
The draws below stay inside these ranges and needn't reach their ends.
Inputs may be any that keep to these rules, and one draw needn't show every extreme that they name: `log_decay`: entries are negative.
All inputs are finite; a program needn't handle non-finite values.
Results may differ from the reference program's by a relative error of at most 0.00035.
Values sent between devices are 32-bit elements; how exact they have to be, the bound alone decides.
No kernel may reach another device: no remote copies, remote signals or barrier semaphores. Data moves between devices by JAX's collectives and lax.ppermute only.
A program may use at most 128 MiB of HBM per device.

```python
import math
import jax
import jax.numpy as jnp
from jax import lax

HEADS = 64
HEAD_DIM = 128
STATE = 128
BLOCK = 512
TOK_DEV = 1024
TOKEN_COUNT = 32768


def draw_log_decay(key, part):
    split_random_keys = jax.random.split(key, 7)
    slow_flag = jax.random.randint(split_random_keys[0], (HEADS, 1), 0, 2).astype(jnp.float32)
    slow_rate = jax.random.uniform(split_random_keys[1], (HEADS, 1), jnp.float32, 0.05, 0.3) * (math.log(10.0) / TOKEN_COUNT)
    fast_rate = jax.random.uniform(split_random_keys[2], (HEADS, 1), jnp.float32, 1.0 / 50.0, 1.0 / 30.0)
    baseline_rate = slow_flag * slow_rate + (1.0 - slow_flag) * fast_rate
    jaggedness = jnp.exp(jax.random.uniform(split_random_keys[3], (HEADS, TOKEN_COUNT), jnp.float32, -0.69, 0.69))
    shard_count = TOKEN_COUNT // TOK_DEV
    per_device_factor = jnp.repeat(jax.random.uniform(split_random_keys[4], (1, shard_count), jnp.float32, 0.5, 1.5), TOK_DEV, axis=1)
    spike_positions = jax.random.randint(split_random_keys[5], (2,), 0, TOKEN_COUNT)
    spike_depth = jax.random.uniform(split_random_keys[6], (2,), jnp.float32, 0.22, 0.69)
    locations = jnp.arange(TOKEN_COUNT)
    spike_events = jnp.sum(jnp.where(locations[None, :] == spike_positions[:, None], spike_depth[:, None], 0.0), axis=0)
    return -(baseline_rate * jaggedness * per_device_factor) - spike_events[None, :]


def shard_levels(own_key, extent, cuts, low, high):
    factor_of = 1.0
    for dim, blocks in cuts:
        draws = jax.random.uniform(jax.random.fold_in(jax.random.fold_in(own_key, 6), dim), (blocks,), jnp.float32, low / len(cuts), high / len(cuts))
        factor_of = factor_of * jnp.repeat(jnp.exp(draws), extent[dim] // blocks).reshape((-1,) + (1,) * (len(extent) - 1 - dim))
    return factor_of


def noise(stream_key, dims, width, limit, shards=(), held_as=jnp.bfloat16):
    result = width * jax.random.normal(stream_key, dims, jnp.float32)
    if shards:
        result = result * shard_levels(stream_key, dims, shards, -0.22, 0.18)
    return jnp.clip(result, -limit, limit).astype(held_as)


def setup_inputs(seed: int = 0) -> dict:
    streams_of = jax.random.split(jax.random.key(seed), 6)
    inputs = noise(streams_of[0], (TOKEN_COUNT, HEADS * HEAD_DIM), 1.0, 6.0, ((0, 32), (1, 16)))
    in_map = noise(streams_of[1], (TOKEN_COUNT, STATE), (STATE ** -0.5), 1.25, ((0, 32),))
    out_map = noise(streams_of[2], (TOKEN_COUNT, STATE), (STATE ** -0.5), 1.25, ((0, 32),))
    log_decay = draw_log_decay(jax.random.fold_in(streams_of[5], 71), 0)
    cotangent = noise(streams_of[4], (TOKEN_COUNT, HEADS * HEAD_DIM), 0.03, 0.4375, ((0, 32), (1, 16)))
    return dict(inputs=inputs, in_map=in_map, out_map=out_map, log_decay=log_decay, cotangent=cotangent)


highest = lax.Precision.HIGHEST

def block_forward(state, pieces):
    inputs_blk, in_blk, out_blk, rates = pieces
    stretch = rates.shape[1]
    locations = jnp.arange(stretch)
    causal = (locations[:, None] >= locations[None, :])[None]
    running = jnp.cumsum(rates, axis=1)
    gaps = running[:, :, None] - running[:, None, :]
    decays = jnp.where(causal, jnp.exp(jnp.where(causal, gaps, 0.0)), 0.0)
    scores = jnp.dot(out_blk, in_blk.T, precision=highest, preferred_element_type=jnp.float32)
    inside = jnp.einsum('hts,shp->thp', decays * scores[None], inputs_blk, precision=highest)
    outside = jnp.einsum('tn,hpn->thp', out_blk, state, precision=highest) * jnp.exp(running).T[:, :, None]
    to_end = jnp.exp(running[:, -1:] - running)
    new_state = jnp.exp(running[:, -1])[:, None, None] * state + jnp.einsum('shp,sn->hpn', inputs_blk * to_end.T[:, :, None], in_blk, precision=highest)
    return (new_state, inside + outside)

def forward(inputs, in_map, out_map, log_decay):
    stretch = min(BLOCK, 128)
    pieces_count = TOKEN_COUNT // stretch
    inputs_blocks = inputs.reshape(pieces_count, stretch, HEADS, HEAD_DIM)
    in_blocks = in_map.reshape(pieces_count, stretch, STATE)
    out_blocks = out_map.reshape(pieces_count, stretch, STATE)
    rate_blocks = log_decay.reshape(HEADS, pieces_count, stretch).transpose(1, 0, 2)
    initial = jnp.zeros((HEADS, HEAD_DIM, STATE), jnp.float32)
    final_state, outputs = lax.scan(jax.checkpoint(block_forward), initial, (inputs_blocks, in_blocks, out_blocks, rate_blocks))
    return outputs.reshape(TOKEN_COUNT, HEADS * HEAD_DIM)

def reference(inputs, in_map, out_map, log_decay, cotangent):
    outputs, pullback = jax.vjp(forward, inputs.astype(jnp.float32), in_map.astype(jnp.float32), out_map.astype(jnp.float32), log_decay)
    grads = pullback(cotangent.astype(jnp.float32))
    return (grads[0], grads[1], grads[2], grads[3])
```

```python
import jax
import jax.numpy as jnp
from jax import lax
from jax.experimental import pallas as pl
from jax.experimental.pallas import tpu as pltpu
from jax.sharding import Mesh, PartitionSpec as P

f32, bf16 = jnp.float32, jnp.bfloat16
SEQ, HEAD = ("x", "z"), ("y", "core")
TOK, HEADS, DIM, TILE = 1024, 4, 128, 128
BLOCKS = TOK // TILE
VMEM = 56 << 20


def dot(a, b, dims):
    return lax.dot_general(a, b, (dims, ((), ())), preferred_element_type=f32)


def split(v):
    hi = v.astype(bf16)
    return hi, (v - hi.astype(f32)).astype(bf16)


def dot_wide(wide, exact):
    return dot(jnp.concatenate(split(wide), axis=1), jnp.concatenate([exact, exact], axis=0), ((1,), (0,)))


def running_sums(v, width, shift_suffix=True):
    lanes = v.shape[1]
    at = lax.broadcasted_iota(jnp.int32, v.shape, 1) & (width - 1)
    prefix = v
    suffix = jnp.where(at < width - 1, pltpu.roll(v, lanes - 1, 1), 0.0) if shift_suffix else v
    step = 1
    while step < width:
        prefix = prefix + jnp.where(at >= step, pltpu.roll(prefix, step, 1), 0.0)
        suffix = suffix + jnp.where(at < width - step, pltpu.roll(suffix, lanes - step, 1), 0.0)
        step *= 2
    return prefix, suffix


def state_kernel(x_ref, dy_ref, b_ref, c_ref, rate_ref, piece_ref, rows_ref):
    rates = jnp.concatenate([rate_ref[...], rate_ref[...]], axis=0)
    prefix, suffix = running_sums(rates, TOK)
    row = lax.broadcasted_iota(jnp.int32, rates.shape, 0)
    rows = jnp.exp(jnp.where(row < HEADS, suffix, prefix))
    rows_ref[...] = rows
    totals = jnp.broadcast_to(jnp.exp(prefix[:, TOK - 1 :]), (8, DIM))
    pair = (totals, jnp.concatenate([totals[2:], totals[:2]], axis=0))
    for k in range(32):
        piece_ref[k, 32:40, :] = pair[k % 2]
    maps = (b_ref[...].astype(f32).T, c_ref[...].astype(f32).T)
    for h in range(HEADS):
        for d, ref in enumerate((x_ref, dy_ref)):
            scaled = maps[d] * rows[d * HEADS + h : d * HEADS + h + 1]
            both = dot(jnp.concatenate(split(scaled), axis=0), ref[:, h * DIM : (h + 1) * DIM], ((1,), (0,)))
            state = both[:DIM] + both[DIM:]
            at = (d * 2 + h % 2) * 8
            for k in range(16):
                piece_ref[2 * k + h // 2, at : at + 8, :] = state[8 * k : 8 * k + 8]


def scan_kernel(got_ref, out_ref):
    for half in range(2):
        at = half * 8
        held = jnp.zeros((8, DIM), f32)
        for k in range(32):
            out_ref[k, at : at + 8, :] = held
            held = held * got_ref[k, 32 + half : 33 + half, :] + got_ref[k, at : at + 8, :]
        at = 16 + half * 8
        held = jnp.zeros((8, DIM), f32)
        for k in reversed(range(32)):
            out_ref[k, at : at + 8, :] = held
            held = held * got_ref[k, 32 + half : 33 + half, :] + got_ref[k, at : at + 8, :]


def piece_of(got_ref, d, h):
    at = (d * 2 + h % 2) * 8
    return jnp.concatenate([got_ref[2 * k + h // 2, at : at + 8, :] for k in range(16)], axis=0)


def local_kernel(first, x_ref, dy_ref, b_ref, c_ref, rate_ref, *refs):
    if first == 0:
        rows_ref, gx_ref, maps_ref, decay_ref, cols_ref, rb, sb, tb, rs, acc, ec = refs
        maps_ref[...] = jnp.zeros(maps_ref.shape, f32)
    else:
        before_ref, gx_ref, maps_ref, decay_ref, rb, sb, tb, rs, acc, ec = refs
        maps_ref[...] = before_ref[...]
    rates = jnp.concatenate([rate_ref[...], rate_ref[...]], axis=0)
    prefix, suffix = running_sums(rates, TILE)
    for k in range(BLOCKS):
        rb[k] = prefix[:, k * TILE : (k + 1) * TILE]
        sb[k] = suffix[:, k * TILE : (k + 1) * TILE]
        tb[k] = jnp.broadcast_to(prefix[:, (k + 1) * TILE - 1 : (k + 1) * TILE], (8, TILE))
        if first == 0:
            rows = rows_ref[:, k * TILE : (k + 1) * TILE]
            cols_ref[k * TILE : (k + 1) * TILE, :] = jnp.concatenate([rows] * 16, axis=0).T
    rs[...] = jnp.zeros(rs.shape, f32)
    causal = lax.broadcasted_iota(jnp.int32, (TILE, TILE), 0) <= lax.broadcasted_iota(jnp.int32, (TILE, TILE), 1)

    def pair(j, i, decays, new):
        sj = pl.ds(pl.multiple_of(j * TILE, TILE), TILE)
        si = pl.ds(pl.multiple_of(i * TILE, TILE), TILE)
        b, c = b_ref[sj, :], c_ref[si, :]
        scores = dot(b, c, ((1,), (1,)))
        joint = None
        for k in range(2):
            lanes = slice(k * DIM, (k + 1) * DIM)
            dy = dy_ref[si, lanes]
            decay = decays(k)
            pairs = dot(x_ref[sj, lanes], dy, ((1,), (1,)))
            weights = decay * scores
            mine = decay * pairs
            joint = mine if joint is None else joint + mine
            product = weights * pairs
            gx = dot_wide(weights, dy)
            if new:
                gx_ref[sj, lanes] = gx
                acc[k] = product
            else:
                gx_ref[sj, lanes] += gx
                acc[k] += product
            rs[i, k : k + 1, :] += jnp.sum(product, axis=0, keepdims=True)
        maps_ref[sj, :DIM] += dot_wide(joint, c)
        maps_ref[si, DIM:] += dot_wide(joint.T, b)

    def outer(j, nothing):
        own, rest = rb[j], sb[j]

        def inside(k):
            across = jnp.broadcast_to(own[first + k : first + k + 1], (TILE, TILE))
            return jnp.where(causal, jnp.exp(across - across.T), 0.0)

        pair(j, j, inside, True)
        for k in range(2):
            ec[k] = jnp.broadcast_to(jnp.exp(rest[first + k : first + k + 1]), (TILE, TILE)).T

        def inner(i, between):
            from_start = jnp.exp(rb[i] + between)
            pair(j, i, lambda k: ec[k] * from_start[first + k : first + k + 1], False)
            return between + tb[i]

        lax.fori_loop(j + 1, BLOCKS, inner, jnp.zeros((8, TILE), f32))
        for k in range(2):
            decay_ref[j, k : k + 1, :] = jnp.sum(acc[k].T, axis=0, keepdims=True)
        return nothing

    lax.fori_loop(0, BLOCKS, outer, 0)
    for k in range(BLOCKS):
        decay_ref[k, 0:2, :] = decay_ref[k, 0:2, :] - rs[k, 0:2, :]


def twice(v):
    return jnp.concatenate([v, v], axis=1)


def maps_kernel(core_ref, got_ref, x_ref, dy_ref, cols_ref, local_ref, keep_ref, send_ref, parts):
    @pl.when(pl.program_id(0) == 0)
    def _():
        for d in range(2):
            for h in range(HEADS):
                parts[d * HEADS + h] = jnp.concatenate(split(piece_of(got_ref, d, h)), axis=1)

    grads = []
    for d, ref in ((1, x_ref), (0, dy_ref)):
        total = local_ref[:, (1 - d) * DIM : (2 - d) * DIM]
        for h in range(HEADS):
            at = (1 - d) * HEADS + h
            fed = dot(twice(ref[:, h * DIM : (h + 1) * DIM]), parts[d * HEADS + h], ((1,), (1,)))
            total = total + cols_ref[:, at : at + 1] * fed
        grads.append(total)
    for core in range(2):
        for there in (core, 1 - core):
            out = keep_ref if there == core else send_ref

            @pl.when(core_ref[0] == core)
            def _():
                for k in range(out.shape[0]):
                    at = (2 * k + there) * 64
                    out[k, :, :DIM] = grads[0][at : at + 64]
                    out[k, :, DIM:] = grads[1][at : at + 64]


def rest_kernel(got_ref, x_ref, dy_ref, b_ref, c_ref, cols_ref, rows_ref, gxa_ref, gxb_ref, da_ref, db_ref,
                gx_ref, decay_ref, parts, stacked, sums):
    step = pl.program_id(0)
    tile = x_ref.shape[0]

    @pl.when(step == 0)
    def _():
        for h in range(HEADS):
            for d in range(2):
                parts[d * HEADS + h] = jnp.concatenate(split(piece_of(got_ref, d, h)), axis=1)
            stacked[h] = jnp.concatenate(split(piece_of(got_ref, 1, h)), axis=0)

    b, c = b_ref[...], c_ref[...]
    wide_b, wide_c = b.astype(f32), c.astype(f32)
    for h in range(HEADS):
        lanes = slice(h * DIM, (h + 1) * DIM)
        local = (gxa_ref, gxb_ref)[h // 2][:, (h % 2) * DIM : (h % 2 + 1) * DIM]
        gx_ref[:, lanes] = local + cols_ref[:, h : h + 1] * dot(twice(b), stacked[h], ((1,), (0,)))
        fed = dot(twice(x_ref[:, lanes]), parts[HEADS + h], ((1,), (1,))) * wide_b
        sums[step, h : h + 1, :] = jnp.sum(fed.T, axis=0, keepdims=True)
        fed = dot(twice(dy_ref[:, lanes]), parts[h], ((1,), (1,))) * wide_c
        sums[step, HEADS + h : HEADS + h + 1, :] = jnp.sum(fed.T, axis=0, keepdims=True)

    @pl.when(step == TOK // tile - 1)
    def _():
        rows = rows_ref[...]
        terms = jnp.concatenate([sums[k] for k in range(TOK // tile)], axis=1) * rows
        local = [jnp.concatenate([ref[k, 0:2, :] for k in range(BLOCKS)], axis=1) for ref in (da_ref, db_ref)]
        terms = terms + jnp.concatenate(local + [jnp.zeros((HEADS, TOK), f32)], axis=0)
        at = lax.broadcasted_iota(jnp.int32, terms.shape, 1)
        moved = jnp.where(at >= 1, pltpu.roll(terms, 1, 1), 0.0)
        prefix, _ = running_sums(moved, TOK, False)
        _, suffix = running_sums(terms, TOK, False)
        decay = prefix[:HEADS] + suffix[HEADS:]
        which = lax.broadcasted_iota(jnp.int32, (HEADS, 1), 0)
        crossing = jnp.zeros((HEADS, 1), f32)
        for h in range(HEADS):
            both = jnp.sum(piece_of(got_ref, 0, h) * piece_of(got_ref, 1, h), axis=0, keepdims=True)
            both = jnp.sum(both, axis=1, keepdims=True)
            crossing = jnp.where(which == h, both, crossing)
        decay_ref[...] = decay + crossing * rows[HEADS:, TOK - 1 :]


def params():
    return pltpu.CompilerParams(vmem_limit_bytes=VMEM)


def shape(*dims, dtype=f32):
    return jax.ShapeDtypeStruct(dims, dtype)


def whole(*dims):
    return pl.BlockSpec(dims, lambda *_: (0,) * len(dims))


def local_pairs(first, x, dy, b, c, rates, other):
    half = pl.BlockSpec((TOK, 2 * DIM), lambda *_: (0, first // 2))
    outs = [shape(TOK, 2 * DIM), shape(TOK, 2 * DIM), shape(BLOCKS, 8, TILE)]
    if first == 0:
        outs.append(shape(TOK, DIM))
    return pl.pallas_call(
        lambda *refs: local_kernel(first, *refs),
        grid=(1,),
        in_specs=[half, half, whole(TOK, DIM), whole(TOK, DIM), whole(HEADS, TOK), whole(*other.shape)],
        out_specs=[whole(*o.shape) for o in outs],
        out_shape=outs,
        scratch_shapes=[pltpu.VMEM((BLOCKS, 8, TILE), f32)] * 4 + [pltpu.VMEM((2, TILE, TILE), f32)] * 2,
        compiler_params=params(),
        name=f"local_{first}",
    )(x, dy, b, c, rates, other)


def on_device(inputs, in_map, out_map, log_decay, cotangent):
    pieces, rows = pl.pallas_call(
        state_kernel,
        out_shape=[shape(32, 40, DIM), shape(8, TOK)],
        compiler_params=params(),
        name="states",
    )(inputs, cotangent, in_map, out_map, log_decay)
    got = lax.all_to_all(pieces, SEQ, 0, 0)
    gx_a, maps, decay_a, cols = local_pairs(0, inputs, cotangent, in_map, out_map, log_decay, rows)
    got, maps = lax.optimization_barrier((got, maps))
    scanned = pl.pallas_call(
        scan_kernel, out_shape=shape(32, 32, DIM), compiler_params=params(), name="scan"
    )(got)
    scanned, maps = lax.optimization_barrier((scanned, maps))
    got = lax.all_to_all(scanned, SEQ, 0, 0)
    gx_b, maps, decay_b = local_pairs(2, inputs, cotangent, in_map, out_map, log_decay, maps)
    got, maps = lax.optimization_barrier((got, maps))
    tile = 256
    steps = TOK // tile
    parts = pltpu.VMEM((2 * HEADS, DIM, 2 * DIM), bf16)
    heads = pl.BlockSpec((tile, HEADS * DIM), lambda i: (i, 0))
    pair = pl.BlockSpec((tile, 2 * DIM), lambda i: (i, 0))
    one = pl.BlockSpec((tile, DIM), lambda i: (i, 0))
    piece = whole(32, 32, DIM)
    core = lax.axis_index("core").astype(jnp.int32).reshape(1)
    rows_of = pl.BlockSpec((steps // 2, 64, 2 * DIM), lambda i: (i, 0, 0))
    keep, send = pl.pallas_call(
        maps_kernel,
        grid=(steps,),
        in_specs=[pl.BlockSpec(memory_space=pltpu.SMEM), piece, heads, heads, one, pair],
        out_specs=[rows_of, rows_of],
        out_shape=[shape(8, 64, 2 * DIM)] * 2,
        scratch_shapes=[parts],
        compiler_params=params(),
        name="maps",
    )(core, got, inputs, cotangent, cols, maps)
    reduced = keep + lax.ppermute(send, "core", [(0, 1), (1, 0)])
    reduced, got = lax.optimization_barrier((reduced, got))
    reduced = lax.all_to_all(reduced, "y", 0, 0)
    grad_inputs, grad_decay = pl.pallas_call(
        rest_kernel,
        grid=(steps,),
        in_specs=[
            piece, heads, heads, one, one, one, whole(8, TOK), pair, pair,
            whole(BLOCKS, 8, TILE), whole(BLOCKS, 8, TILE),
        ],
        out_specs=[heads, whole(HEADS, TOK)],
        out_shape=[shape(TOK, HEADS * DIM), shape(HEADS, TOK)],
        scratch_shapes=[parts, pltpu.VMEM((HEADS, 2 * DIM, DIM), bf16), pltpu.VMEM((steps, 8, tile), f32)],
        compiler_params=params(),
        name="rest",
    )(got, inputs, cotangent, in_map, out_map, cols, rows, gx_a, gx_b, decay_a, decay_b)
    reduced, grad_decay = lax.optimization_barrier((reduced, grad_decay))
    total = jnp.sum(reduced, axis=0)
    return (grad_inputs, total[:, :DIM], total[:, DIM:], grad_decay)


def solution(mesh):
    grid = Mesh(mesh.devices.reshape(4, 8, 8, 2), SEQ + HEAD)
    rows, columns = P(SEQ, None), P(SEQ, HEAD)
    return jax.shard_map(
        on_device,
        mesh=grid,
        in_specs=(columns, rows, rows, P(HEAD, SEQ), columns),
        out_specs=(columns, P(SEQ + HEAD, None), P(SEQ + HEAD, None), P(HEAD, SEQ)),
        check_vma=False,
    )
```

```python
import jax
import jax.numpy as jnp
from jax import lax
from jax.experimental import pallas as pl
from jax.experimental.pallas import tpu as pltpu
from jax.sharding import Mesh, PartitionSpec as P

f32, bf16 = jnp.float32, jnp.bfloat16
SEQ, HEAD = ("x", "z"), ("y", "core")
TOK, HEADS, DIM, TILE = 1024, 4, 128, 128
BLOCKS = TOK // TILE
STATES, LOCAL, SCAN, MAPS, REST = 56, 24, 4, 12, 16


def dot(a, b, dims):
    return lax.dot_general(a, b, (dims, ((), ())), preferred_element_type=f32)


def split(v):
    hi = v.astype(bf16)
    return hi, (v - hi.astype(f32)).astype(bf16)


def dot_wide(wide, exact):
    return dot(jnp.concatenate(split(wide), axis=1), jnp.concatenate([exact, exact], axis=0), ((1,), (0,)))


def running_sums(v, width, shift_suffix=True):
    lanes = v.shape[1]
    at = lax.broadcasted_iota(jnp.int32, v.shape, 1) & (width - 1)
    prefix = v
    suffix = jnp.where(at < width - 1, pltpu.roll(v, lanes - 1, 1), 0.0) if shift_suffix else v
    step = 1
    while step < width:
        prefix = prefix + jnp.where(at >= step, pltpu.roll(prefix, step, 1), 0.0)
        suffix = suffix + jnp.where(at < width - step, pltpu.roll(suffix, lanes - step, 1), 0.0)
        step *= 2
    return prefix, suffix


def state_kernel(x_ref, dy_ref, b_ref, c_ref, rate_ref, piece_ref, rows_ref, turned, total):
    step = pl.program_id(0)

    @pl.when(step == 0)
    def _():
        rates = jnp.concatenate([rate_ref[...], rate_ref[...]], axis=0)
        prefix, suffix = running_sums(rates, TOK)
        row = lax.broadcasted_iota(jnp.int32, rates.shape, 0)
        rows_ref[...] = jnp.exp(jnp.where(row < HEADS, suffix, prefix))
        totals = jnp.broadcast_to(jnp.exp(prefix[:, TOK - 1 :]), (8, DIM))
        total[0] = totals
        total[1] = jnp.concatenate([totals[2:], totals[:2]], axis=0)
        turned[0] = b_ref[...].astype(f32).T
        turned[1] = c_ref[...].astype(f32).T

    for k in range(16):
        piece_ref[k, 0, 32:40, :] = total[step]
    for h in range(2):
        for d, ref in enumerate((x_ref, dy_ref)):
            scaled = turned[d] * rows_ref[pl.ds(d * HEADS + 2 * step + h, 1), :]
            both = dot(jnp.concatenate(split(scaled), axis=0), ref[:, h * DIM : (h + 1) * DIM], ((1,), (0,)))
            state = both[:DIM] + both[DIM:]
            at = (d * 2 + h) * 8
            for k in range(16):
                piece_ref[k, 0, at : at + 8, :] = state[8 * k : 8 * k + 8]


def scan_kernel(got_ref, out_ref):
    for d in range(2):

        @pl.when(pl.program_id(0) == d)
        def _():
            for half in range(2):
                at = half * 8
                held = jnp.zeros((8, DIM), f32)
                for k in range(32) if d == 0 else reversed(range(32)):
                    out_ref[k, at : at + 8, :] = held
                    part = got_ref[k, d * 16 + at : d * 16 + at + 8, :]
                    held = held * got_ref[k, 32 + half : 33 + half, :] + part


def piece_of(got_ref, d, h):
    at = (d * 2 + h % 2) * 8
    return jnp.concatenate([got_ref[2 * k + h // 2, at : at + 8, :] for k in range(16)], axis=0)


def block_sums(rate_ref, rb, sb, tb):
    rates = jnp.concatenate([rate_ref[...], rate_ref[...]], axis=0)
    prefix, suffix = running_sums(rates, TILE)
    for k in range(BLOCKS):
        rb[k] = prefix[:, k * TILE : (k + 1) * TILE]
        sb[k] = suffix[:, k * TILE : (k + 1) * TILE]
        if tb is not None:
            tb[k] = jnp.broadcast_to(jnp.exp(prefix[:, (k + 1) * TILE - 1 : (k + 1) * TILE]), (8, TILE))


def local_kernel(x_ref, dy_ref, b_ref, c_ref, rate_ref, rows_ref, gx_ref, work_ref, decay_ref,
                 rb, sb, tb, ro, part, held_ref):
    block_sums(rate_ref, rb, sb, tb)
    causal = lax.broadcasted_iota(jnp.int32, (TILE, TILE), 0) <= lax.broadcasted_iota(jnp.int32, (TILE, TILE), 1)

    def block(j, nothing):
        at = pl.ds(pl.multiple_of(j * TILE, TILE), TILE)
        b, c, own = b_ref[at, :], c_ref[at, :], rb[j]
        scores = dot(b, c, ((1,), (1,)))
        scales = (jnp.exp(sb[j]), jnp.exp(own))
        turned = (b.astype(f32).T, c.astype(f32).T)
        joint = None
        for h in range(HEADS):
            lanes = slice(h * DIM, (h + 1) * DIM)
            x, dy = x_ref[at, lanes], dy_ref[at, lanes]
            across = jnp.broadcast_to(own[h : h + 1], (TILE, TILE))
            decay = jnp.where(causal, jnp.exp(across - across.T), 0.0)
            pairs = dot(x, dy, ((1,), (1,)))
            weights = decay * scores
            mine = decay * pairs
            joint = mine if joint is None else joint + mine
            product = weights * pairs
            gx_ref[at, lanes] = dot_wide(weights, dy)
            decay_ref[j, h : h + 1, :] = jnp.sum(product.T - product, axis=0, keepdims=True)
            for d, from_ in enumerate((x, dy)):
                wide = jnp.concatenate(split(turned[d] * scales[d][h : h + 1]), axis=0)
                both = dot(wide, from_, ((1,), (0,)))
                part[j, d * HEADS + h] = both[:DIM] + both[DIM:]
        work_ref[at, :DIM] = dot_wide(joint, c)
        work_ref[at, DIM : 2 * DIM] = dot_wide(joint.T, b)
        return nothing

    lax.fori_loop(0, BLOCKS, block, 0)
    for d in range(2):
        for h in range(HEADS):
            held = jnp.zeros((TILE, DIM), f32)
            for k in range(BLOCKS) if d == 0 else reversed(range(BLOCKS)):
                held_ref[k, d * HEADS + h] = jnp.concatenate(split(held), axis=1)
                held = held * tb[k, h : h + 1, :] + part[k, d * HEADS + h]
    for k in range(BLOCKS):
        ro[k] = rows_ref[:, k * TILE : (k + 1) * TILE]

    def carried(j, nothing):
        at = pl.ds(pl.multiple_of(j * TILE, TILE), TILE)
        b, c = b_ref[at, :], c_ref[at, :]
        wide_b, wide_c = b.astype(f32), c.astype(f32)
        scale = jnp.concatenate([jnp.exp(sb[j, 0:HEADS, :]), jnp.exp(rb[j, 0:HEADS, :])], axis=0)
        cols = jnp.concatenate([scale, ro[j]] * 8, axis=0).T
        work_ref[at, 2 * DIM :] = cols
        grad_in, grad_out = work_ref[at, :DIM], work_ref[at, DIM : 2 * DIM]
        for h in range(HEADS):
            lanes = slice(h * DIM, (h + 1) * DIM)
            after = held_ref[j, HEADS + h]
            to_end = jnp.broadcast_to(cols[:, h : h + 1], (TILE, DIM))
            stacked = jnp.concatenate([after[:, :DIM], after[:, DIM:]], axis=0)
            gx_ref[at, lanes] += to_end * dot(twice(b), stacked, ((1,), (0,)))
            fed_in = to_end * dot(twice(x_ref[at, lanes]), after, ((1,), (1,)))
            fed_out = cols[:, HEADS + h : HEADS + h + 1] * dot(twice(dy_ref[at, lanes]), held_ref[j, h], ((1,), (1,)))
            grad_in = grad_in + fed_in
            grad_out = grad_out + fed_out
            change = fed_in * wide_b - fed_out * wide_c
            decay_ref[j, h : h + 1, :] += jnp.sum(change.T, axis=0, keepdims=True)
        work_ref[at, :DIM] = grad_in
        work_ref[at, DIM : 2 * DIM] = grad_out
        return nothing

    lax.fori_loop(0, BLOCKS, carried, 0)


def twice(v):
    return jnp.concatenate([v, v], axis=1)


def maps_kernel(core_ref, got_ref, x_ref, dy_ref, work_ref, keep_ref, send_ref, parts):
    @pl.when(pl.program_id(0) == 0)
    def _():
        for d in range(2):
            for h in range(HEADS):
                parts[d * HEADS + h] = jnp.concatenate(split(piece_of(got_ref, d, h)), axis=1)

    grads = []
    for d, ref in ((1, x_ref), (0, dy_ref)):
        total = work_ref[:, (1 - d) * DIM : (2 - d) * DIM]
        for h in range(HEADS):
            at = 2 * DIM + 8 + (1 - d) * HEADS + h
            fed = dot(twice(ref[:, h * DIM : (h + 1) * DIM]), parts[d * HEADS + h], ((1,), (1,)))
            total = total + work_ref[:, at : at + 1] * fed
        grads.append(total)
    for core in range(2):
        for there in (core, 1 - core):
            out = keep_ref if there == core else send_ref

            @pl.when(core_ref[0] == core)
            def _():
                for k in range(out.shape[0]):
                    at = (2 * k + there) * 64
                    out[k, :, :DIM] = grads[0][at : at + 64]
                    out[k, :, DIM:] = grads[1][at : at + 64]


def rest_kernel(got_ref, x_ref, dy_ref, b_ref, c_ref, cols_ref, rows_ref, gx0_ref, decay0_ref,
                gx_ref, decay_ref, parts, stacked, sums):
    step = pl.program_id(0)
    tile = x_ref.shape[0]

    @pl.when(step == 0)
    def _():
        for h in range(HEADS):
            for d in range(2):
                parts[d * HEADS + h] = jnp.concatenate(split(piece_of(got_ref, d, h)), axis=1)
            stacked[h] = jnp.concatenate(split(piece_of(got_ref, 1, h)), axis=0)

    b, c = b_ref[...], c_ref[...]
    wide_b, wide_c = b.astype(f32), c.astype(f32)
    for h in range(HEADS):
        lanes = slice(h * DIM, (h + 1) * DIM)
        gx_ref[:, lanes] = gx0_ref[:, lanes] + cols_ref[:, 8 + h : 9 + h] * dot(twice(b), stacked[h], ((1,), (0,)))
        fed = dot(twice(x_ref[:, lanes]), parts[HEADS + h], ((1,), (1,))) * wide_b
        sums[step, h : h + 1, :] = jnp.sum(fed.T, axis=0, keepdims=True)
        fed = dot(twice(dy_ref[:, lanes]), parts[h], ((1,), (1,))) * wide_c
        sums[step, HEADS + h : HEADS + h + 1, :] = jnp.sum(fed.T, axis=0, keepdims=True)

    @pl.when(step == TOK // tile - 1)
    def _():
        rows = rows_ref[...]
        terms = jnp.concatenate([sums[k] for k in range(TOK // tile)], axis=1) * rows
        local = jnp.concatenate([decay0_ref[k, 0:HEADS, :] for k in range(BLOCKS)], axis=1)
        terms = terms + jnp.concatenate([local, jnp.zeros((HEADS, TOK), f32)], axis=0)
        at = lax.broadcasted_iota(jnp.int32, terms.shape, 1)
        moved = jnp.where(at >= 1, pltpu.roll(terms, 1, 1), 0.0)
        prefix, _ = running_sums(moved, TOK, False)
        _, suffix = running_sums(terms, TOK, False)
        decay = prefix[:HEADS] + suffix[HEADS:]
        which = lax.broadcasted_iota(jnp.int32, (HEADS, 1), 0)
        crossing = jnp.zeros((HEADS, 1), f32)
        for h in range(HEADS):
            both = jnp.sum(piece_of(got_ref, 0, h) * piece_of(got_ref, 1, h), axis=0, keepdims=True)
            both = jnp.sum(both, axis=1, keepdims=True)
            crossing = jnp.where(which == h, both, crossing)
        decay_ref[...] = decay + crossing * rows[HEADS:, TOK - 1 :]


def sum_kernel(parts_ref, in_ref, out_ref):
    total = parts_ref[0]
    for k in range(1, parts_ref.shape[0]):
        total = total + parts_ref[k]
    in_ref[...] = total[:, :DIM]
    out_ref[...] = total[:, DIM:]


def params(mib):
    return pltpu.CompilerParams(vmem_limit_bytes=mib << 20)


def shape(*dims, dtype=f32):
    return jax.ShapeDtypeStruct(dims, dtype)


def whole(*dims):
    return pl.BlockSpec(dims, lambda *_: (0,) * len(dims))


def on_device(inputs, in_map, out_map, log_decay, cotangent):
    half = pl.BlockSpec((TOK, 2 * DIM), lambda i: (0, i))
    pieces, rows = pl.pallas_call(
        state_kernel,
        grid=(2,),
        in_specs=[half, half, whole(TOK, DIM), whole(TOK, DIM), whole(HEADS, TOK)],
        out_specs=[pl.BlockSpec((16, 1, 40, DIM), lambda i: (0, i, 0, 0)), whole(8, TOK)],
        out_shape=[shape(16, 2, 40, DIM), shape(8, TOK)],
        scratch_shapes=[pltpu.VMEM((2, DIM, TOK), f32), pltpu.VMEM((2, 8, DIM), f32)],
        compiler_params=params(STATES),
        name="states",
    )(inputs, cotangent, in_map, out_map, log_decay)
    got = lax.all_to_all(pieces.reshape(32, 40, DIM), SEQ, 0, 0)
    sums = pltpu.VMEM((BLOCKS, 8, TILE), f32)
    gx, work, decay = pl.pallas_call(
        local_kernel,
        out_shape=[shape(TOK, HEADS * DIM), shape(TOK, 3 * DIM), shape(BLOCKS, 8, TILE)],
        scratch_shapes=[sums] * 4
        + [pltpu.VMEM((BLOCKS, 2 * HEADS, DIM, DIM), f32), pltpu.VMEM((BLOCKS, 2 * HEADS, DIM, 2 * DIM), bf16)],
        compiler_params=params(LOCAL),
        name="local",
    )(inputs, cotangent, in_map, out_map, log_decay, rows)
    got, work = lax.optimization_barrier((got, work))
    scanned = pl.pallas_call(
        scan_kernel,
        grid=(2,),
        in_specs=[whole(32, 40, DIM)],
        out_specs=pl.BlockSpec((32, 16, DIM), lambda i: (0, i, 0)),
        out_shape=pltpu.HBM((32, 32, DIM), f32),
        compiler_params=params(SCAN),
        name="scan",
    )(got)
    got = lax.all_to_all(scanned, SEQ, 0, 0)
    tile = 256
    steps = TOK // tile
    parts = pltpu.VMEM((2 * HEADS, DIM, 2 * DIM), bf16)
    heads = pl.BlockSpec((tile, HEADS * DIM), lambda i: (i, 0))
    one = pl.BlockSpec((tile, DIM), lambda i: (i, 0))
    piece = whole(32, 32, DIM)
    core = lax.axis_index("core").astype(jnp.int32).reshape(1)
    rows_of = pl.BlockSpec((steps // 2, 64, 2 * DIM), lambda i: (i, 0, 0))
    keep, send = pl.pallas_call(
        maps_kernel,
        grid=(steps,),
        in_specs=[pl.BlockSpec(memory_space=pltpu.SMEM), piece, heads, heads, pl.BlockSpec((tile, 3 * DIM), lambda i: (i, 0))],
        out_specs=[rows_of, rows_of],
        out_shape=[shape(8, 64, 2 * DIM)] * 2,
        scratch_shapes=[parts],
        compiler_params=params(MAPS),
        name="maps",
    )(core, got, inputs, cotangent, pltpu.with_memory_space_constraint(work, pltpu.HBM))
    reduced = keep + lax.ppermute(send, "core", [(0, 1), (1, 0)])
    reduced, got = lax.optimization_barrier((reduced, got))
    reduced = lax.all_to_all(reduced, "y", 0, 0)
    grad_inputs, grad_decay = pl.pallas_call(
        rest_kernel,
        grid=(steps,),
        in_specs=[
            piece, heads, heads, one, one, pl.BlockSpec((tile, DIM), lambda i: (i, 2)), whole(8, TOK), heads,
            whole(BLOCKS, 8, TILE),
        ],
        out_specs=[heads, whole(HEADS, TOK)],
        out_shape=[shape(TOK, HEADS * DIM), shape(HEADS, TOK)],
        scratch_shapes=[parts, pltpu.VMEM((HEADS, 2 * DIM, DIM), bf16), pltpu.VMEM((steps, 8, tile), f32)],
        compiler_params=params(REST),
        name="rest",
    )(got, inputs, cotangent, in_map, out_map, work, rows, gx, decay)
    reduced, grad_decay = lax.optimization_barrier((reduced, grad_decay))
    grad_in_map, grad_out_map = pl.pallas_call(
        sum_kernel, out_shape=[shape(64, DIM)] * 2, compiler_params=params(SCAN), name="sum"
    )(reduced)
    return (grad_inputs, grad_in_map, grad_out_map, grad_decay)


def solution(mesh):
    grid = Mesh(mesh.devices.reshape(4, 8, 8, 2), SEQ + HEAD)
    rows, columns = P(SEQ, None), P(SEQ, HEAD)
    return jax.shard_map(
        on_device,
        mesh=grid,
        in_specs=(columns, rows, rows, P(HEAD, SEQ), columns),
        out_specs=(columns, P(SEQ + HEAD, None), P(SEQ + HEAD, None), P(HEAD, SEQ)),
        check_vma=False,
    )
```

```python
import jax
import jax.numpy as jnp
from jax import lax
from jax.experimental import pallas as pl
from jax.experimental.pallas import tpu as pltpu
from jax.sharding import Mesh, PartitionSpec as P

f32, bf16 = jnp.float32, jnp.bfloat16
SEQ, HEAD = ("x", "z"), ("y", "core")
TOK, HEADS, DIM, TILE = 1024, 4, 128, 128
BLOCKS = TOK // TILE
STATES, LOCAL, SCAN, MAPS, REST = 56, 24, 4, 12, 10


def dot(a, b, dims):
    return lax.dot_general(a, b, (dims, ((), ())), preferred_element_type=f32)


def split(v):
    hi = v.astype(bf16)
    return hi, (v - hi.astype(f32)).astype(bf16)


def dot_wide(wide, exact):
    return dot(jnp.concatenate(split(wide), axis=1), jnp.concatenate([exact, exact], axis=0), ((1,), (0,)))


def running_sums(v, width, shift_suffix=True):
    lanes = v.shape[1]
    at = lax.broadcasted_iota(jnp.int32, v.shape, 1) & (width - 1)
    prefix = v
    suffix = jnp.where(at < width - 1, pltpu.roll(v, lanes - 1, 1), 0.0) if shift_suffix else v
    step = 1
    while step < width:
        prefix = prefix + jnp.where(at >= step, pltpu.roll(prefix, step, 1), 0.0)
        suffix = suffix + jnp.where(at < width - step, pltpu.roll(suffix, lanes - step, 1), 0.0)
        step *= 2
    return prefix, suffix


def state_kernel(x_ref, dy_ref, b_ref, c_ref, rate_ref, piece_ref, rows_ref, turned, total):
    step = pl.program_id(0)

    @pl.when(step == 0)
    def _():
        rates = jnp.concatenate([rate_ref[...], rate_ref[...]], axis=0)
        prefix, suffix = running_sums(rates, TOK)
        row = lax.broadcasted_iota(jnp.int32, rates.shape, 0)
        rows_ref[...] = jnp.exp(jnp.where(row < HEADS, suffix, prefix))
        totals = jnp.broadcast_to(jnp.exp(prefix[:, TOK - 1 :]), (8, DIM))
        total[0] = totals
        total[1] = jnp.concatenate([totals[2:], totals[:2]], axis=0)
        turned[0] = b_ref[...].astype(f32).T
        turned[1] = c_ref[...].astype(f32).T

    for k in range(16):
        piece_ref[k, 0, 32:40, :] = total[step]
    for h in range(2):
        for d, ref in enumerate((x_ref, dy_ref)):
            scaled = turned[d] * rows_ref[pl.ds(d * HEADS + 2 * step + h, 1), :]
            both = dot(jnp.concatenate(split(scaled), axis=0), ref[:, h * DIM : (h + 1) * DIM], ((1,), (0,)))
            state = both[:DIM] + both[DIM:]
            at = (d * 2 + h) * 8
            for k in range(16):
                piece_ref[k, 0, at : at + 8, :] = state[8 * k : 8 * k + 8]


def scan_kernel(got_ref, out_ref):
    for d in range(2):

        @pl.when(pl.program_id(0) == d)
        def _():
            for half in range(2):
                at = half * 8
                held = jnp.zeros((8, DIM), f32)
                for k in range(32) if d == 0 else reversed(range(32)):
                    out_ref[k, at : at + 8, :] = held
                    part = got_ref[k, d * 16 + at : d * 16 + at + 8, :]
                    held = held * got_ref[k, 32 + half : 33 + half, :] + part


def piece_of(got_ref, d, h):
    at = (d * 2 + h % 2) * 8
    return jnp.concatenate([got_ref[2 * k + h // 2, at : at + 8, :] for k in range(16)], axis=0)


def columns(rows):
    return jnp.concatenate([jnp.concatenate([rows[:, k : k + TILE]] * 16, axis=0).T for k in range(0, rows.shape[1], TILE)], axis=0)


def sort_rows(core_ref, rows_ref, keep_ref, send_ref):
    own = pl.multiple_of(core_ref[0] * 64, 64)
    for k in range(keep_ref.shape[0]):
        keep_ref[k] = rows_ref[pl.ds(k * 128 + own, 64), :]
        send_ref[k] = rows_ref[pl.ds(k * 128 + 64 - own, 64), :]


def block_sums(rate_ref, rb, sb, tb):
    rates = jnp.concatenate([rate_ref[...], rate_ref[...]], axis=0)
    prefix, suffix = running_sums(rates, TILE)
    for k in range(BLOCKS):
        rb[k] = prefix[:, k * TILE : (k + 1) * TILE]
        sb[k] = suffix[:, k * TILE : (k + 1) * TILE]
        if tb is not None:
            tb[k] = jnp.broadcast_to(jnp.exp(prefix[:, (k + 1) * TILE - 1 : (k + 1) * TILE]), (8, TILE))


def local_kernel(core_ref, x_ref, dy_ref, b_ref, c_ref, rate_ref, gx_ref, keep_ref, send_ref, decay_ref,
                 rb, sb, tb, part, held_ref, work_ref):
    block_sums(rate_ref, rb, sb, tb)
    causal = lax.broadcasted_iota(jnp.int32, (TILE, TILE), 0) <= lax.broadcasted_iota(jnp.int32, (TILE, TILE), 1)

    def block(j, nothing):
        at = pl.ds(pl.multiple_of(j * TILE, TILE), TILE)
        b, c, own = b_ref[at, :], c_ref[at, :], rb[j]
        scores = dot(b, c, ((1,), (1,)))
        scales = (jnp.exp(sb[j]), jnp.exp(own))
        turned = (b.astype(f32).T, c.astype(f32).T)
        joint = None
        for h in range(HEADS):
            lanes = slice(h * DIM, (h + 1) * DIM)
            x, dy = x_ref[at, lanes], dy_ref[at, lanes]
            across = jnp.broadcast_to(own[h : h + 1], (TILE, TILE))
            decay = jnp.where(causal, jnp.exp(across - across.T), 0.0)
            pairs = dot(x, dy, ((1,), (1,)))
            weights = decay * scores
            mine = decay * pairs
            joint = mine if joint is None else joint + mine
            product = weights * pairs
            gx_ref[at, lanes] = dot_wide(weights, dy)
            decay_ref[j, h : h + 1, :] = jnp.sum(product.T - product, axis=0, keepdims=True)
            for d, from_ in enumerate((x, dy)):
                wide = jnp.concatenate(split(turned[d] * scales[d][h : h + 1]), axis=0)
                both = dot(wide, from_, ((1,), (0,)))
                part[j, d * HEADS + h] = both[:DIM] + both[DIM:]
        work_ref[at, :DIM] = dot_wide(joint, c)
        work_ref[at, DIM : 2 * DIM] = dot_wide(joint.T, b)
        return nothing

    lax.fori_loop(0, BLOCKS, block, 0)
    for d in range(2):
        for h in range(HEADS):
            held = jnp.zeros((TILE, DIM), f32)
            for k in range(BLOCKS) if d == 0 else reversed(range(BLOCKS)):
                held_ref[k, d * HEADS + h] = jnp.concatenate(split(held), axis=1)
                held = held * tb[k, h : h + 1, :] + part[k, d * HEADS + h]
    def carried(j, nothing):
        at = pl.ds(pl.multiple_of(j * TILE, TILE), TILE)
        b, c = b_ref[at, :], c_ref[at, :]
        wide_b, wide_c = b.astype(f32), c.astype(f32)
        scale = jnp.concatenate([jnp.exp(sb[j, 0:HEADS, :]), jnp.exp(rb[j, 0:HEADS, :])], axis=0)
        cols = columns(scale)
        grad_in, grad_out = work_ref[at, :DIM], work_ref[at, DIM : 2 * DIM]
        for h in range(HEADS):
            lanes = slice(h * DIM, (h + 1) * DIM)
            after = held_ref[j, HEADS + h]
            to_end = jnp.broadcast_to(cols[:, h : h + 1], (TILE, DIM))
            stacked = jnp.concatenate([after[:, :DIM], after[:, DIM:]], axis=0)
            gx_ref[at, lanes] += to_end * dot(twice(b), stacked, ((1,), (0,)))
            fed_in = to_end * dot(twice(x_ref[at, lanes]), after, ((1,), (1,)))
            fed_out = cols[:, HEADS + h : HEADS + h + 1] * dot(twice(dy_ref[at, lanes]), held_ref[j, h], ((1,), (1,)))
            grad_in = grad_in + fed_in
            grad_out = grad_out + fed_out
            change = fed_in * wide_b - fed_out * wide_c
            decay_ref[j, h : h + 1, :] += jnp.sum(change.T, axis=0, keepdims=True)
        work_ref[at, :DIM] = grad_in
        work_ref[at, DIM : 2 * DIM] = grad_out
        return nothing

    lax.fori_loop(0, BLOCKS, carried, 0)
    sort_rows(core_ref, work_ref, keep_ref, send_ref)


def twice(v):
    return jnp.concatenate([v, v], axis=1)


def maps_kernel(core_ref, got_ref, x_ref, dy_ref, rows_ref, keep_ref, send_ref, parts, work):
    @pl.when(pl.program_id(0) == 0)
    def _():
        for d in range(2):
            for h in range(HEADS):
                parts[d * HEADS + h] = jnp.concatenate(split(piece_of(got_ref, d, h)), axis=1)

    cols = columns(rows_ref[...])
    for d, ref in ((1, x_ref), (0, dy_ref)):
        total = None
        for h in range(HEADS):
            at = (1 - d) * HEADS + h
            fed = dot(twice(ref[:, h * DIM : (h + 1) * DIM]), parts[d * HEADS + h], ((1,), (1,)))
            fed = cols[:, at : at + 1] * fed
            total = fed if total is None else total + fed
        work[:, (1 - d) * DIM : (2 - d) * DIM] = total
    sort_rows(core_ref, work, keep_ref, send_ref)


def rest_kernel(got_ref, x_ref, dy_ref, b_ref, c_ref, tile_rows_ref, rows_ref, gx0_ref, decay0_ref,
                gx_ref, decay_ref, parts, stacked, sums):
    step = pl.program_id(0)
    tile = x_ref.shape[0]

    @pl.when(step == 0)
    def _():
        for h in range(HEADS):
            for d in range(2):
                parts[d * HEADS + h] = jnp.concatenate(split(piece_of(got_ref, d, h)), axis=1)
            stacked[h] = jnp.concatenate(split(piece_of(got_ref, 1, h)), axis=0)

    b, c = b_ref[...], c_ref[...]
    wide_b, wide_c = b.astype(f32), c.astype(f32)
    cols = columns(tile_rows_ref[...])
    for h in range(HEADS):
        lanes = slice(h * DIM, (h + 1) * DIM)
        gx_ref[:, lanes] = gx0_ref[:, lanes] + cols[:, h : h + 1] * dot(twice(b), stacked[h], ((1,), (0,)))
        fed = dot(twice(x_ref[:, lanes]), parts[HEADS + h], ((1,), (1,))) * wide_b
        sums[step, h : h + 1, :] = jnp.sum(fed.T, axis=0, keepdims=True)
        fed = dot(twice(dy_ref[:, lanes]), parts[h], ((1,), (1,))) * wide_c
        sums[step, HEADS + h : HEADS + h + 1, :] = jnp.sum(fed.T, axis=0, keepdims=True)

    @pl.when(step == TOK // tile - 1)
    def _():
        rows = rows_ref[...]
        terms = jnp.concatenate([sums[k] for k in range(TOK // tile)], axis=1) * rows
        local = jnp.concatenate([decay0_ref[k, 0:HEADS, :] for k in range(BLOCKS)], axis=1)
        terms = terms + jnp.concatenate([local, jnp.zeros((HEADS, TOK), f32)], axis=0)
        at = lax.broadcasted_iota(jnp.int32, terms.shape, 1)
        moved = jnp.where(at >= 1, pltpu.roll(terms, 1, 1), 0.0)
        prefix, _ = running_sums(moved, TOK, False)
        _, suffix = running_sums(terms, TOK, False)
        decay = prefix[:HEADS] + suffix[HEADS:]
        which = lax.broadcasted_iota(jnp.int32, (HEADS, 1), 0)
        crossing = jnp.zeros((HEADS, 1), f32)
        for h in range(HEADS):
            both = jnp.sum(piece_of(got_ref, 0, h) * piece_of(got_ref, 1, h), axis=0, keepdims=True)
            both = jnp.sum(both, axis=1, keepdims=True)
            crossing = jnp.where(which == h, both, crossing)
        decay_ref[...] = decay + crossing * rows[HEADS:, TOK - 1 :]


def sum_kernel(parts_ref, in_ref, out_ref):
    total = parts_ref[0]
    for k in range(1, parts_ref.shape[0]):
        total = total + parts_ref[k]
    in_ref[...] = total[:, :DIM]
    out_ref[...] = total[:, DIM:]


def params(mib):
    return pltpu.CompilerParams(vmem_limit_bytes=mib << 20)


def shape(*dims, dtype=f32):
    return jax.ShapeDtypeStruct(dims, dtype)


def whole(*dims):
    return pl.BlockSpec(dims, lambda *_: (0,) * len(dims))


def on_device(inputs, in_map, out_map, log_decay, cotangent):
    half = pl.BlockSpec((TOK, 2 * DIM), lambda i: (0, i))
    pieces, rows = pl.pallas_call(
        state_kernel,
        grid=(2,),
        in_specs=[half, half, whole(TOK, DIM), whole(TOK, DIM), whole(HEADS, TOK)],
        out_specs=[pl.BlockSpec((16, 1, 40, DIM), lambda i: (0, i, 0, 0)), whole(8, TOK)],
        out_shape=[shape(16, 2, 40, DIM), shape(8, TOK)],
        scratch_shapes=[pltpu.VMEM((2, DIM, TOK), f32), pltpu.VMEM((2, 8, DIM), f32)],
        compiler_params=params(STATES),
        name="states",
    )(inputs, cotangent, in_map, out_map, log_decay)
    got = lax.all_to_all(pieces.reshape(32, 40, DIM), SEQ, 0, 0)
    sums = pltpu.VMEM((BLOCKS, 8, TILE), f32)
    core = lax.axis_index("core").astype(jnp.int32).reshape(1)
    scalar = pl.BlockSpec(memory_space=pltpu.SMEM)
    sorted_rows = shape(8, 64, 2 * DIM)
    gx, keep_near, send_near, decay = pl.pallas_call(
        local_kernel,
        in_specs=[scalar] + [whole(*v.shape) for v in (inputs, cotangent, in_map, out_map, log_decay)],
        out_shape=[shape(TOK, HEADS * DIM), sorted_rows, sorted_rows, shape(BLOCKS, 8, TILE)],
        scratch_shapes=[sums] * 3
        + [
            pltpu.VMEM((BLOCKS, 2 * HEADS, DIM, DIM), f32),
            pltpu.VMEM((BLOCKS, 2 * HEADS, DIM, 2 * DIM), bf16),
            pltpu.VMEM((TOK, 2 * DIM), f32),
        ],
        compiler_params=params(LOCAL),
        name="local",
    )(core, inputs, cotangent, in_map, out_map, log_decay)
    got, send_near = lax.optimization_barrier((got, send_near))
    scanned = pl.pallas_call(
        scan_kernel,
        grid=(2,),
        in_specs=[whole(32, 40, DIM)],
        out_specs=pl.BlockSpec((32, 16, DIM), lambda i: (0, i, 0)),
        out_shape=pltpu.HBM((32, 32, DIM), f32),
        compiler_params=params(SCAN),
        name="scan",
    )(got)
    scanned, send_near = lax.optimization_barrier((scanned, send_near))
    got = lax.all_to_all(scanned, SEQ, 0, 0)
    swap = [(0, 1), (1, 0)]
    near = keep_near + lax.ppermute(send_near, "core", swap)
    got, near = lax.optimization_barrier((got, near))
    tile = 256
    steps = TOK // tile
    parts = pltpu.VMEM((2 * HEADS, DIM, 2 * DIM), bf16)
    heads = pl.BlockSpec((tile, HEADS * DIM), lambda i: (i, 0))
    one = pl.BlockSpec((tile, DIM), lambda i: (i, 0))
    piece = whole(32, 32, DIM)
    tile_rows = pl.BlockSpec((8, tile), lambda i: (0, i))
    rows_of = pl.BlockSpec((steps // 2, 64, 2 * DIM), lambda i: (i, 0, 0))
    keep, send = pl.pallas_call(
        maps_kernel,
        grid=(steps,),
        in_specs=[scalar, piece, heads, heads, tile_rows],
        out_specs=[rows_of, rows_of],
        out_shape=[sorted_rows] * 2,
        scratch_shapes=[parts, pltpu.VMEM((tile, 2 * DIM), f32)],
        compiler_params=params(MAPS),
        name="maps",
    )(core, got, inputs, cotangent, rows)
    reduced = keep + near + lax.ppermute(send, "core", swap)
    reduced, got = lax.optimization_barrier((reduced, got))
    reduced = lax.all_to_all(reduced, "y", 0, 0)
    grad_inputs, grad_decay = pl.pallas_call(
        rest_kernel,
        grid=(steps,),
        in_specs=[
            piece, heads, heads, one, one, tile_rows, whole(8, TOK), heads,
            whole(BLOCKS, 8, TILE),
        ],
        out_specs=[heads, whole(HEADS, TOK)],
        out_shape=[shape(TOK, HEADS * DIM), shape(HEADS, TOK)],
        scratch_shapes=[parts, pltpu.VMEM((HEADS, 2 * DIM, DIM), bf16), pltpu.VMEM((steps, 8, tile), f32)],
        compiler_params=params(REST),
        name="rest",
    )(got, inputs, cotangent, in_map, out_map, rows, rows, gx, decay)
    reduced, grad_decay = lax.optimization_barrier((reduced, grad_decay))
    grad_in_map, grad_out_map = pl.pallas_call(
        sum_kernel, out_shape=[shape(64, DIM)] * 2, compiler_params=params(SCAN), name="sum"
    )(reduced)
    return (grad_inputs, grad_in_map, grad_out_map, grad_decay)


def solution(mesh):
    grid = Mesh(mesh.devices.reshape(4, 8, 8, 2), SEQ + HEAD)
    rows, columns = P(SEQ, None), P(SEQ, HEAD)
    return jax.shard_map(
        on_device,
        mesh=grid,
        in_specs=(columns, rows, rows, P(HEAD, SEQ), columns),
        out_specs=(columns, P(SEQ + HEAD, None), P(SEQ + HEAD, None), P(HEAD, SEQ)),
        check_vma=False,
    )
```

```python
import jax
import jax.numpy as jnp
from jax import lax
from jax.experimental import pallas as pl
from jax.experimental.pallas import tpu as pltpu
from jax.sharding import Mesh, PartitionSpec as P

f32, bf16 = jnp.float32, jnp.bfloat16
SEQ, HEAD = ("x", "z"), ("y", "core")
TOK, HEADS, DIM, TILE = 1024, 4, 128, 128
BLOCKS = TOK // TILE
STATES, LOCAL, SCAN, MAPS, REST = 56, 24, 4, 12, 10


def dot(a, b, dims):
    return lax.dot_general(a, b, (dims, ((), ())), preferred_element_type=f32)


def split(v):
    hi = v.astype(bf16)
    return hi, (v - hi.astype(f32)).astype(bf16)


def dot_wide(wide, exact):
    return dot(jnp.concatenate(split(wide), axis=1), jnp.concatenate([exact, exact], axis=0), ((1,), (0,)))


def running_sums(v, width, shift_suffix=True):
    lanes = v.shape[1]
    at = lax.broadcasted_iota(jnp.int32, v.shape, 1) & (width - 1)
    prefix = v
    suffix = jnp.where(at < width - 1, pltpu.roll(v, lanes - 1, 1), 0.0) if shift_suffix else v
    step = 1
    while step < width:
        prefix = prefix + jnp.where(at >= step, pltpu.roll(prefix, step, 1), 0.0)
        suffix = suffix + jnp.where(at < width - step, pltpu.roll(suffix, lanes - step, 1), 0.0)
        step *= 2
    return prefix, suffix


def state_kernel(x_ref, dy_ref, b_ref, c_ref, rate_ref, piece_ref, rows_ref, turned, total):
    step = pl.program_id(0)

    @pl.when(step == 0)
    def _():
        rates = jnp.concatenate([rate_ref[...], rate_ref[...]], axis=0)
        prefix, suffix = running_sums(rates, TOK)
        row = lax.broadcasted_iota(jnp.int32, rates.shape, 0)
        rows_ref[...] = jnp.exp(jnp.where(row < HEADS, suffix, prefix))
        totals = jnp.broadcast_to(jnp.exp(prefix[:, TOK - 1 :]), (8, DIM))
        total[0] = totals
        total[1] = jnp.concatenate([totals[2:], totals[:2]], axis=0)
        turned[0] = b_ref[...].astype(f32).T
        turned[1] = c_ref[...].astype(f32).T

    for k in range(16):
        piece_ref[k, 0, 8] = total[step, 0:4, :]
    for h in range(2):
        for d, ref in enumerate((x_ref, dy_ref)):
            scaled = turned[d] * rows_ref[pl.ds(d * HEADS + 2 * step + h, 1), :]
            both = dot(jnp.concatenate(split(scaled), axis=0), ref[:, h * DIM : (h + 1) * DIM], ((1,), (0,)))
            state = both[:DIM] + both[DIM:]
            at = (d * 2 + h) * 2
            for k in range(16):
                piece_ref[k, 0, at] = state[8 * k : 8 * k + 4]
                piece_ref[k, 0, at + 1] = state[8 * k + 4 : 8 * k + 8]


def scan_kernel(got_ref, out_ref):
    for d in range(2):

        @pl.when(pl.program_id(0) == d)
        def _():
            for at in range(0, 16, 4):
                held = jnp.zeros((4, DIM), f32)
                for k in range(32) if d == 0 else reversed(range(32)):
                    out_ref[k, at : at + 4, :] = held
                    held = held * got_ref[k, 8, at // 8 : at // 8 + 1, :] + got_ref[k, d * 4 + at // 4]


def piece_of(got_ref, d, h):
    at = (d * 2 + h % 2) * 8
    return jnp.concatenate([got_ref[2 * k + h // 2, at : at + 8, :] for k in range(16)], axis=0)


def columns(rows):
    return jnp.concatenate([jnp.concatenate([rows[:, k : k + TILE]] * 16, axis=0).T for k in range(0, rows.shape[1], TILE)], axis=0)


def sort_rows(core_ref, rows_ref, keep_ref, send_ref):
    own = pl.multiple_of(core_ref[0] * 64, 64)
    for k in range(keep_ref.shape[0]):
        keep_ref[k] = rows_ref[pl.ds(k * 128 + own, 64), :]
        send_ref[k] = rows_ref[pl.ds(k * 128 + 64 - own, 64), :]


def block_sums(rate_ref, rb, sb, tb):
    rates = jnp.concatenate([rate_ref[...], rate_ref[...]], axis=0)
    prefix, suffix = running_sums(rates, TILE)
    for k in range(BLOCKS):
        rb[k] = prefix[:, k * TILE : (k + 1) * TILE]
        sb[k] = suffix[:, k * TILE : (k + 1) * TILE]
        if tb is not None:
            tb[k] = jnp.broadcast_to(jnp.exp(prefix[:, (k + 1) * TILE - 1 : (k + 1) * TILE]), (8, TILE))


def local_kernel(core_ref, x_ref, dy_ref, b_ref, c_ref, rate_ref, gx_ref, keep_ref, send_ref, decay_ref,
                 rb, sb, tb, part, held_ref, work_ref):
    block_sums(rate_ref, rb, sb, tb)
    causal = lax.broadcasted_iota(jnp.int32, (TILE, TILE), 0) <= lax.broadcasted_iota(jnp.int32, (TILE, TILE), 1)

    def block(j, nothing):
        at = pl.ds(pl.multiple_of(j * TILE, TILE), TILE)
        b, c, own = b_ref[at, :], c_ref[at, :], rb[j]
        scores = dot(b, c, ((1,), (1,)))
        scales = (jnp.exp(sb[j]), jnp.exp(own))
        turned = (b.astype(f32).T, c.astype(f32).T)
        joint = None
        for h in range(HEADS):
            lanes = slice(h * DIM, (h + 1) * DIM)
            x, dy = x_ref[at, lanes], dy_ref[at, lanes]
            across = jnp.broadcast_to(own[h : h + 1], (TILE, TILE))
            decay = jnp.where(causal, jnp.exp(across - across.T), 0.0)
            pairs = dot(x, dy, ((1,), (1,)))
            weights = decay * scores
            mine = decay * pairs
            joint = mine if joint is None else joint + mine
            product = weights * pairs
            gx_ref[at, lanes] = dot_wide(weights, dy)
            decay_ref[j, h : h + 1, :] = jnp.sum(product.T - product, axis=0, keepdims=True)
            for d, from_ in enumerate((x, dy)):
                wide = jnp.concatenate(split(turned[d] * scales[d][h : h + 1]), axis=0)
                both = dot(wide, from_, ((1,), (0,)))
                part[j, d * HEADS + h] = both[:DIM] + both[DIM:]
        work_ref[at, :DIM] = dot_wide(joint, c)
        work_ref[at, DIM : 2 * DIM] = dot_wide(joint.T, b)
        return nothing

    lax.fori_loop(0, BLOCKS, block, 0)
    for d in range(2):
        for h in range(HEADS):
            held = jnp.zeros((TILE, DIM), f32)
            for k in range(BLOCKS) if d == 0 else reversed(range(BLOCKS)):
                held_ref[k, d * HEADS + h] = jnp.concatenate(split(held), axis=1)
                held = held * tb[k, h : h + 1, :] + part[k, d * HEADS + h]
    def carried(j, nothing):
        at = pl.ds(pl.multiple_of(j * TILE, TILE), TILE)
        b, c = b_ref[at, :], c_ref[at, :]
        wide_b, wide_c = b.astype(f32), c.astype(f32)
        scale = jnp.concatenate([jnp.exp(sb[j, 0:HEADS, :]), jnp.exp(rb[j, 0:HEADS, :])], axis=0)
        cols = columns(scale)
        grad_in, grad_out = work_ref[at, :DIM], work_ref[at, DIM : 2 * DIM]
        for h in range(HEADS):
            lanes = slice(h * DIM, (h + 1) * DIM)
            after = held_ref[j, HEADS + h]
            to_end = jnp.broadcast_to(cols[:, h : h + 1], (TILE, DIM))
            stacked = jnp.concatenate([after[:, :DIM], after[:, DIM:]], axis=0)
            gx_ref[at, lanes] += to_end * dot(twice(b), stacked, ((1,), (0,)))
            fed_in = to_end * dot(twice(x_ref[at, lanes]), after, ((1,), (1,)))
            fed_out = cols[:, HEADS + h : HEADS + h + 1] * dot(twice(dy_ref[at, lanes]), held_ref[j, h], ((1,), (1,)))
            grad_in = grad_in + fed_in
            grad_out = grad_out + fed_out
            change = fed_in * wide_b - fed_out * wide_c
            decay_ref[j, h : h + 1, :] += jnp.sum(change.T, axis=0, keepdims=True)
        work_ref[at, :DIM] = grad_in
        work_ref[at, DIM : 2 * DIM] = grad_out
        return nothing

    lax.fori_loop(0, BLOCKS, carried, 0)
    sort_rows(core_ref, work_ref, keep_ref, send_ref)


def twice(v):
    return jnp.concatenate([v, v], axis=1)


def maps_kernel(core_ref, got_ref, x_ref, dy_ref, rows_ref, keep_ref, send_ref, parts, work):
    @pl.when(pl.program_id(0) == 0)
    def _():
        for d in range(2):
            for h in range(HEADS):
                parts[d * HEADS + h] = jnp.concatenate(split(piece_of(got_ref, d, h)), axis=1)

    cols = columns(rows_ref[...])
    for d, ref in ((1, x_ref), (0, dy_ref)):
        total = None
        for h in range(HEADS):
            at = (1 - d) * HEADS + h
            fed = dot(twice(ref[:, h * DIM : (h + 1) * DIM]), parts[d * HEADS + h], ((1,), (1,)))
            fed = cols[:, at : at + 1] * fed
            total = fed if total is None else total + fed
        work[:, (1 - d) * DIM : (2 - d) * DIM] = total
    sort_rows(core_ref, work, keep_ref, send_ref)


def rest_kernel(got_ref, x_ref, dy_ref, b_ref, c_ref, tile_rows_ref, rows_ref, gx0_ref, decay0_ref,
                gx_ref, decay_ref, parts, stacked, sums):
    step = pl.program_id(0)
    tile = x_ref.shape[0]

    @pl.when(step == 0)
    def _():
        for h in range(HEADS):
            for d in range(2):
                parts[d * HEADS + h] = jnp.concatenate(split(piece_of(got_ref, d, h)), axis=1)
            stacked[h] = jnp.concatenate(split(piece_of(got_ref, 1, h)), axis=0)

    b, c = b_ref[...], c_ref[...]
    wide_b, wide_c = b.astype(f32), c.astype(f32)
    cols = columns(tile_rows_ref[...])
    for h in range(HEADS):
        lanes = slice(h * DIM, (h + 1) * DIM)
        gx_ref[:, lanes] = gx0_ref[:, lanes] + cols[:, h : h + 1] * dot(twice(b), stacked[h], ((1,), (0,)))
        fed = dot(twice(x_ref[:, lanes]), parts[HEADS + h], ((1,), (1,))) * wide_b
        sums[step, h : h + 1, :] = jnp.sum(fed.T, axis=0, keepdims=True)
        fed = dot(twice(dy_ref[:, lanes]), parts[h], ((1,), (1,))) * wide_c
        sums[step, HEADS + h : HEADS + h + 1, :] = jnp.sum(fed.T, axis=0, keepdims=True)

    @pl.when(step == TOK // tile - 1)
    def _():
        rows = rows_ref[...]
        terms = jnp.concatenate([sums[k] for k in range(TOK // tile)], axis=1) * rows
        local = jnp.concatenate([decay0_ref[k, 0:HEADS, :] for k in range(BLOCKS)], axis=1)
        terms = terms + jnp.concatenate([local, jnp.zeros((HEADS, TOK), f32)], axis=0)
        at = lax.broadcasted_iota(jnp.int32, terms.shape, 1)
        moved = jnp.where(at >= 1, pltpu.roll(terms, 1, 1), 0.0)
        prefix, _ = running_sums(moved, TOK, False)
        _, suffix = running_sums(terms, TOK, False)
        decay = prefix[:HEADS] + suffix[HEADS:]
        which = lax.broadcasted_iota(jnp.int32, (HEADS, 1), 0)
        crossing = jnp.zeros((HEADS, 1), f32)
        for h in range(HEADS):
            both = jnp.sum(piece_of(got_ref, 0, h) * piece_of(got_ref, 1, h), axis=0, keepdims=True)
            both = jnp.sum(both, axis=1, keepdims=True)
            crossing = jnp.where(which == h, both, crossing)
        decay_ref[...] = decay + crossing * rows[HEADS:, TOK - 1 :]


def sum_kernel(parts_ref, in_ref, out_ref):
    total = parts_ref[0]
    for k in range(1, parts_ref.shape[0]):
        total = total + parts_ref[k]
    in_ref[...] = total[:, :DIM]
    out_ref[...] = total[:, DIM:]


def params(mib):
    return pltpu.CompilerParams(vmem_limit_bytes=mib << 20)


def shape(*dims, dtype=f32):
    return jax.ShapeDtypeStruct(dims, dtype)


def whole(*dims):
    return pl.BlockSpec(dims, lambda *_: (0,) * len(dims))


def on_device(inputs, in_map, out_map, log_decay, cotangent):
    half = pl.BlockSpec((TOK, 2 * DIM), lambda i: (0, i))
    pieces, rows = pl.pallas_call(
        state_kernel,
        grid=(2,),
        in_specs=[half, half, whole(TOK, DIM), whole(TOK, DIM), whole(HEADS, TOK)],
        out_specs=[pl.BlockSpec((16, 1, 9, 4, DIM), lambda i: (0, i, 0, 0, 0)), whole(8, TOK)],
        out_shape=[shape(16, 2, 9, 4, DIM), shape(8, TOK)],
        scratch_shapes=[pltpu.VMEM((2, DIM, TOK), f32), pltpu.VMEM((2, 8, DIM), f32)],
        compiler_params=params(STATES),
        name="states",
    )(inputs, cotangent, in_map, out_map, log_decay)
    got = lax.all_to_all(pieces.reshape(32, 9, 4, DIM), SEQ, 0, 0)
    sums = pltpu.VMEM((BLOCKS, 8, TILE), f32)
    core = lax.axis_index("core").astype(jnp.int32).reshape(1)
    scalar = pl.BlockSpec(memory_space=pltpu.SMEM)
    sorted_rows = shape(8, 64, 2 * DIM)
    gx, keep_near, send_near, decay = pl.pallas_call(
        local_kernel,
        in_specs=[scalar] + [whole(*v.shape) for v in (inputs, cotangent, in_map, out_map, log_decay)],
        out_shape=[shape(TOK, HEADS * DIM), sorted_rows, sorted_rows, shape(BLOCKS, 8, TILE)],
        scratch_shapes=[sums] * 3
        + [
            pltpu.VMEM((BLOCKS, 2 * HEADS, DIM, DIM), f32),
            pltpu.VMEM((BLOCKS, 2 * HEADS, DIM, 2 * DIM), bf16),
            pltpu.VMEM((TOK, 2 * DIM), f32),
        ],
        compiler_params=params(LOCAL),
        name="local",
    )(core, inputs, cotangent, in_map, out_map, log_decay)
    got, send_near = lax.optimization_barrier((got, send_near))
    scanned = pl.pallas_call(
        scan_kernel,
        grid=(2,),
        in_specs=[whole(32, 9, 4, DIM)],
        out_specs=pl.BlockSpec((32, 16, DIM), lambda i: (0, i, 0)),
        out_shape=pltpu.HBM((32, 32, DIM), f32),
        compiler_params=params(SCAN),
        name="scan",
    )(got)
    scanned, send_near = lax.optimization_barrier((scanned, send_near))
    got = lax.all_to_all(scanned, SEQ, 0, 0)
    swap = [(0, 1), (1, 0)]
    near = keep_near + lax.ppermute(send_near, "core", swap)
    got, near = lax.optimization_barrier((got, near))
    tile = 256
    steps = TOK // tile
    parts = pltpu.VMEM((2 * HEADS, DIM, 2 * DIM), bf16)
    heads = pl.BlockSpec((tile, HEADS * DIM), lambda i: (i, 0))
    one = pl.BlockSpec((tile, DIM), lambda i: (i, 0))
    piece = whole(32, 32, DIM)
    tile_rows = pl.BlockSpec((8, tile), lambda i: (0, i))
    rows_of = pl.BlockSpec((steps // 2, 64, 2 * DIM), lambda i: (i, 0, 0))
    keep, send = pl.pallas_call(
        maps_kernel,
        grid=(steps,),
        in_specs=[scalar, piece, heads, heads, tile_rows],
        out_specs=[rows_of, rows_of],
        out_shape=[sorted_rows] * 2,
        scratch_shapes=[parts, pltpu.VMEM((tile, 2 * DIM), f32)],
        compiler_params=params(MAPS),
        name="maps",
    )(core, got, inputs, cotangent, rows)
    reduced = keep + near + lax.ppermute(send, "core", swap)
    reduced, got = lax.optimization_barrier((reduced, got))
    reduced = lax.all_to_all(reduced, "y", 0, 0)
    grad_inputs, grad_decay = pl.pallas_call(
        rest_kernel,
        grid=(steps,),
        in_specs=[
            piece, heads, heads, one, one, tile_rows, whole(8, TOK), heads,
            whole(BLOCKS, 8, TILE),
        ],
        out_specs=[heads, whole(HEADS, TOK)],
        out_shape=[shape(TOK, HEADS * DIM), shape(HEADS, TOK)],
        scratch_shapes=[parts, pltpu.VMEM((HEADS, 2 * DIM, DIM), bf16), pltpu.VMEM((steps, 8, tile), f32)],
        compiler_params=params(REST),
        name="rest",
    )(got, inputs, cotangent, in_map, out_map, rows, rows, gx, decay)
    reduced, grad_decay = lax.optimization_barrier((reduced, grad_decay))
    grad_in_map, grad_out_map = pl.pallas_call(
        sum_kernel, out_shape=[shape(64, DIM)] * 2, compiler_params=params(SCAN), name="sum"
    )(reduced)
    return (grad_inputs, grad_in_map, grad_out_map, grad_decay)


def solution(mesh):
    grid = Mesh(mesh.devices.reshape(4, 8, 8, 2), SEQ + HEAD)
    rows, columns = P(SEQ, None), P(SEQ, HEAD)
    return jax.shard_map(
        on_device,
        mesh=grid,
        in_specs=(columns, rows, rows, P(HEAD, SEQ), columns),
        out_specs=(columns, P(SEQ + HEAD, None), P(SEQ + HEAD, None), P(HEAD, SEQ)),
        check_vma=False,
    )
```

```python
import jax
import jax.numpy as jnp
from jax import lax
from jax.experimental import pallas as pl
from jax.experimental.pallas import tpu as pltpu
from jax.sharding import Mesh, PartitionSpec as P

f32, bf16 = jnp.float32, jnp.bfloat16
SEQ, HEAD = ("x", "z"), ("y", "core")
TOK, HEADS, DIM, TILE = 1024, 4, 128, 128
BLOCKS = TOK // TILE
STATES, LOCAL, SCAN, MAPS, REST = 56, 24, 4, 12, 56


def dot(a, b, dims):
    return lax.dot_general(a, b, (dims, ((), ())), preferred_element_type=f32)


def split(v):
    hi = v.astype(bf16)
    return hi, (v - hi.astype(f32)).astype(bf16)


def dot_wide(wide, exact):
    return dot(jnp.concatenate(split(wide), axis=1), jnp.concatenate([exact, exact], axis=0), ((1,), (0,)))


def running_sums(v, width, shift_suffix=True):
    lanes = v.shape[1]
    at = lax.broadcasted_iota(jnp.int32, v.shape, 1) & (width - 1)
    prefix = v
    suffix = jnp.where(at < width - 1, pltpu.roll(v, lanes - 1, 1), 0.0) if shift_suffix else v
    step = 1
    while step < width:
        prefix = prefix + jnp.where(at >= step, pltpu.roll(prefix, step, 1), 0.0)
        suffix = suffix + jnp.where(at < width - step, pltpu.roll(suffix, lanes - step, 1), 0.0)
        step *= 2
    return prefix, suffix


def state_kernel(x_ref, dy_ref, b_ref, c_ref, rate_ref, piece_ref, rows_ref, turned, total):
    step = pl.program_id(0)

    @pl.when(step == 0)
    def _():
        rates = jnp.concatenate([rate_ref[...], rate_ref[...]], axis=0)
        prefix, suffix = running_sums(rates, TOK)
        row = lax.broadcasted_iota(jnp.int32, rates.shape, 0)
        rows_ref[...] = jnp.exp(jnp.where(row < HEADS, suffix, prefix))
        totals = jnp.broadcast_to(jnp.exp(prefix[:, TOK - 1 :]), (8, DIM))
        total[0] = totals
        total[1] = jnp.concatenate([totals[2:], totals[:2]], axis=0)
        turned[0] = b_ref[...].astype(f32).T
        turned[1] = c_ref[...].astype(f32).T

    for k in range(16):
        piece_ref[k, 0, 8] = total[step, 0:4, :]
    for h in range(2):
        for d, ref in enumerate((x_ref, dy_ref)):
            scaled = turned[d] * rows_ref[pl.ds(d * HEADS + 2 * step + h, 1), :]
            both = dot(jnp.concatenate(split(scaled), axis=0), ref[:, h * DIM : (h + 1) * DIM], ((1,), (0,)))
            state = both[:DIM] + both[DIM:]
            at = (d * 2 + h) * 2
            for k in range(16):
                piece_ref[k, 0, at] = state[8 * k : 8 * k + 4]
                piece_ref[k, 0, at + 1] = state[8 * k + 4 : 8 * k + 8]


def scan_kernel(got_ref, out_ref):
    for d in range(2):

        @pl.when(pl.program_id(0) == d)
        def _():
            for at in range(0, 16, 4):
                held = jnp.zeros((4, DIM), f32)
                for k in range(32) if d == 0 else reversed(range(32)):
                    out_ref[k, at : at + 4, :] = held
                    held = held * got_ref[k, 8, at // 8 : at // 8 + 1, :] + got_ref[k, d * 4 + at // 4]


def piece_of(got_ref, d, h):
    at = (d * 2 + h % 2) * 8
    return jnp.concatenate([got_ref[2 * k + h // 2, at : at + 8, :] for k in range(16)], axis=0)


def columns(rows):
    return jnp.concatenate([jnp.concatenate([rows[:, k : k + TILE]] * 16, axis=0).T for k in range(0, rows.shape[1], TILE)], axis=0)


def sort_rows(core_ref, rows_ref, keep_ref, send_ref):
    own = pl.multiple_of(core_ref[0] * 64, 64)
    for k in range(keep_ref.shape[0]):
        keep_ref[k] = rows_ref[pl.ds(k * 128 + own, 64), :]
        send_ref[k] = rows_ref[pl.ds(k * 128 + 64 - own, 64), :]


def block_sums(rate_ref, rb, sb, tb):
    rates = jnp.concatenate([rate_ref[...], rate_ref[...]], axis=0)
    prefix, suffix = running_sums(rates, TILE)
    for k in range(BLOCKS):
        rb[k] = prefix[:, k * TILE : (k + 1) * TILE]
        sb[k] = suffix[:, k * TILE : (k + 1) * TILE]
        if tb is not None:
            tb[k] = jnp.broadcast_to(jnp.exp(prefix[:, (k + 1) * TILE - 1 : (k + 1) * TILE]), (8, TILE))


def local_kernel(core_ref, x_ref, dy_ref, b_ref, c_ref, rate_ref, gx_ref, keep_ref, send_ref, decay_ref,
                 rb, sb, tb, part, held_ref, work_ref):
    block_sums(rate_ref, rb, sb, tb)
    causal = lax.broadcasted_iota(jnp.int32, (TILE, TILE), 0) <= lax.broadcasted_iota(jnp.int32, (TILE, TILE), 1)

    def block(j, nothing):
        at = pl.ds(pl.multiple_of(j * TILE, TILE), TILE)
        b, c, own = b_ref[at, :], c_ref[at, :], rb[j]
        scores = dot(b, c, ((1,), (1,)))
        scales = (jnp.exp(sb[j]), jnp.exp(own))
        turned = (b.astype(f32).T, c.astype(f32).T)
        joint = None
        for h in range(HEADS):
            lanes = slice(h * DIM, (h + 1) * DIM)
            x, dy = x_ref[at, lanes], dy_ref[at, lanes]
            across = jnp.broadcast_to(own[h : h + 1], (TILE, TILE))
            decay = jnp.where(causal, jnp.exp(across - across.T), 0.0)
            pairs = dot(x, dy, ((1,), (1,)))
            weights = decay * scores
            mine = decay * pairs
            joint = mine if joint is None else joint + mine
            product = weights * pairs
            gx_ref[at, lanes] = dot_wide(weights, dy)
            decay_ref[j, h : h + 1, :] = jnp.sum(product.T - product, axis=0, keepdims=True)
            for d, from_ in enumerate((x, dy)):
                wide = jnp.concatenate(split(turned[d] * scales[d][h : h + 1]), axis=0)
                both = dot(wide, from_, ((1,), (0,)))
                part[j, d * HEADS + h] = both[:DIM] + both[DIM:]
        work_ref[at, :DIM] = dot_wide(joint, c)
        work_ref[at, DIM : 2 * DIM] = dot_wide(joint.T, b)
        return nothing

    lax.fori_loop(0, BLOCKS, block, 0)
    for d in range(2):
        for h in range(HEADS):
            held = jnp.zeros((TILE, DIM), f32)
            for k in range(BLOCKS) if d == 0 else reversed(range(BLOCKS)):
                held_ref[k, d * HEADS + h] = jnp.concatenate(split(held), axis=1)
                held = held * tb[k, h : h + 1, :] + part[k, d * HEADS + h]
    def carried(j, nothing):
        at = pl.ds(pl.multiple_of(j * TILE, TILE), TILE)
        b, c = b_ref[at, :], c_ref[at, :]
        wide_b, wide_c = b.astype(f32), c.astype(f32)
        scale = jnp.concatenate([jnp.exp(sb[j, 0:HEADS, :]), jnp.exp(rb[j, 0:HEADS, :])], axis=0)
        cols = columns(scale)
        grad_in, grad_out = work_ref[at, :DIM], work_ref[at, DIM : 2 * DIM]
        for h in range(HEADS):
            lanes = slice(h * DIM, (h + 1) * DIM)
            after = held_ref[j, HEADS + h]
            to_end = jnp.broadcast_to(cols[:, h : h + 1], (TILE, DIM))
            stacked = jnp.concatenate([after[:, :DIM], after[:, DIM:]], axis=0)
            gx_ref[at, lanes] += to_end * dot(twice(b), stacked, ((1,), (0,)))
            fed_in = to_end * dot(twice(x_ref[at, lanes]), after, ((1,), (1,)))
            fed_out = cols[:, HEADS + h : HEADS + h + 1] * dot(twice(dy_ref[at, lanes]), held_ref[j, h], ((1,), (1,)))
            grad_in = grad_in + fed_in
            grad_out = grad_out + fed_out
            change = fed_in * wide_b - fed_out * wide_c
            decay_ref[j, h : h + 1, :] += jnp.sum(change.T, axis=0, keepdims=True)
        work_ref[at, :DIM] = grad_in
        work_ref[at, DIM : 2 * DIM] = grad_out
        return nothing

    lax.fori_loop(0, BLOCKS, carried, 0)
    sort_rows(core_ref, work_ref, keep_ref, send_ref)


def twice(v):
    return jnp.concatenate([v, v], axis=1)


def maps_kernel(core_ref, got_ref, x_ref, dy_ref, rows_ref, keep_ref, send_ref, parts, work):
    @pl.when(pl.program_id(0) == 0)
    def _():
        for d in range(2):
            for h in range(HEADS):
                parts[d * HEADS + h] = jnp.concatenate(split(piece_of(got_ref, d, h)), axis=1)

    cols = columns(rows_ref[...])
    for d, ref in ((1, x_ref), (0, dy_ref)):
        total = None
        for h in range(HEADS):
            at = (1 - d) * HEADS + h
            fed = dot(twice(ref[:, h * DIM : (h + 1) * DIM]), parts[d * HEADS + h], ((1,), (1,)))
            fed = cols[:, at : at + 1] * fed
            total = fed if total is None else total + fed
        work[:, (1 - d) * DIM : (2 - d) * DIM] = total
    sort_rows(core_ref, work, keep_ref, send_ref)


def rest_kernel(got_ref, x_ref, dy_ref, b_ref, c_ref, tile_rows_ref, rows_ref, gx0_ref, decay0_ref,
                gx_ref, decay_ref, parts, stacked, sums):
    step = pl.program_id(0)
    tile = x_ref.shape[0]

    @pl.when(step == 0)
    def _():
        for h in range(HEADS):
            for d in range(2):
                parts[d * HEADS + h] = jnp.concatenate(split(piece_of(got_ref, d, h)), axis=1)
            stacked[h] = jnp.concatenate(split(piece_of(got_ref, 1, h)), axis=0)

    b, c = b_ref[...], c_ref[...]
    wide_b, wide_c = b.astype(f32), c.astype(f32)
    cols = columns(tile_rows_ref[...])
    for h in range(HEADS):
        lanes = slice(h * DIM, (h + 1) * DIM)
        gx_ref[:, lanes] = gx0_ref[:, lanes] + cols[:, h : h + 1] * dot(twice(b), stacked[h], ((1,), (0,)))
        fed = dot(twice(x_ref[:, lanes]), parts[HEADS + h], ((1,), (1,))) * wide_b
        sums[step, h : h + 1, :] = jnp.sum(fed.T, axis=0, keepdims=True)
        fed = dot(twice(dy_ref[:, lanes]), parts[h], ((1,), (1,))) * wide_c
        sums[step, HEADS + h : HEADS + h + 1, :] = jnp.sum(fed.T, axis=0, keepdims=True)

    @pl.when(step == TOK // tile - 1)
    def _():
        rows = rows_ref[...]
        terms = jnp.concatenate([sums[k] for k in range(TOK // tile)], axis=1) * rows
        local = jnp.concatenate([decay0_ref[k, 0:HEADS, :] for k in range(BLOCKS)], axis=1)
        terms = terms + jnp.concatenate([local, jnp.zeros((HEADS, TOK), f32)], axis=0)
        at = lax.broadcasted_iota(jnp.int32, terms.shape, 1)
        moved = jnp.where(at >= 1, pltpu.roll(terms, 1, 1), 0.0)
        prefix, _ = running_sums(moved, TOK, False)
        _, suffix = running_sums(terms, TOK, False)
        decay = prefix[:HEADS] + suffix[HEADS:]
        which = lax.broadcasted_iota(jnp.int32, (HEADS, 1), 0)
        crossing = jnp.zeros((HEADS, 1), f32)
        for h in range(HEADS):
            both = jnp.sum(piece_of(got_ref, 0, h) * piece_of(got_ref, 1, h), axis=0, keepdims=True)
            both = jnp.sum(both, axis=1, keepdims=True)
            crossing = jnp.where(which == h, both, crossing)
        decay_ref[...] = decay + crossing * rows[HEADS:, TOK - 1 :]


def sum_kernel(parts_ref, in_ref, out_ref):
    total = parts_ref[0]
    for k in range(1, parts_ref.shape[0]):
        total = total + parts_ref[k]
    in_ref[...] = total[:, :DIM]
    out_ref[...] = total[:, DIM:]


def params(mib):
    return pltpu.CompilerParams(vmem_limit_bytes=mib << 20)


def shape(*dims, dtype=f32):
    return jax.ShapeDtypeStruct(dims, dtype)


def whole(*dims):
    return pl.BlockSpec(dims, lambda *_: (0,) * len(dims))


def on_device(inputs, in_map, out_map, log_decay, cotangent):
    half = pl.BlockSpec((TOK, 2 * DIM), lambda i: (0, i))
    pieces, rows = pl.pallas_call(
        state_kernel,
        grid=(2,),
        in_specs=[half, half, whole(TOK, DIM), whole(TOK, DIM), whole(HEADS, TOK)],
        out_specs=[pl.BlockSpec((16, 1, 9, 4, DIM), lambda i: (0, i, 0, 0, 0)), whole(8, TOK)],
        out_shape=[shape(16, 2, 9, 4, DIM), shape(8, TOK)],
        scratch_shapes=[pltpu.VMEM((2, DIM, TOK), f32), pltpu.VMEM((2, 8, DIM), f32)],
        compiler_params=params(STATES),
        name="states",
    )(inputs, cotangent, in_map, out_map, log_decay)
    got = lax.all_to_all(pieces.reshape(32, 9, 4, DIM), SEQ, 0, 0)
    sums = pltpu.VMEM((BLOCKS, 8, TILE), f32)
    core = lax.axis_index("core").astype(jnp.int32).reshape(1)
    scalar = pl.BlockSpec(memory_space=pltpu.SMEM)
    sorted_rows = shape(8, 64, 2 * DIM)
    gx, keep_near, send_near, decay = pl.pallas_call(
        local_kernel,
        in_specs=[scalar] + [whole(*v.shape) for v in (inputs, cotangent, in_map, out_map, log_decay)],
        out_shape=[shape(TOK, HEADS * DIM), sorted_rows, sorted_rows, shape(BLOCKS, 8, TILE)],
        scratch_shapes=[sums] * 3
        + [
            pltpu.VMEM((BLOCKS, 2 * HEADS, DIM, DIM), f32),
            pltpu.VMEM((BLOCKS, 2 * HEADS, DIM, 2 * DIM), bf16),
            pltpu.VMEM((TOK, 2 * DIM), f32),
        ],
        compiler_params=params(LOCAL),
        name="local",
    )(core, inputs, cotangent, in_map, out_map, log_decay)
    got, send_near = lax.optimization_barrier((got, send_near))
    scanned = pl.pallas_call(
        scan_kernel,
        grid=(2,),
        in_specs=[whole(32, 9, 4, DIM)],
        out_specs=pl.BlockSpec((32, 16, DIM), lambda i: (0, i, 0)),
        out_shape=pltpu.HBM((32, 32, DIM), f32),
        compiler_params=params(SCAN),
        name="scan",
    )(got)
    scanned, send_near = lax.optimization_barrier((scanned, send_near))
    got = lax.all_to_all(scanned, SEQ, 0, 0)
    swap = [(0, 1), (1, 0)]
    near = keep_near + lax.ppermute(send_near, "core", swap)
    got, near = lax.optimization_barrier((got, near))
    tile = 256
    steps = TOK // tile
    parts = pltpu.VMEM((2 * HEADS, DIM, 2 * DIM), bf16)
    heads = pl.BlockSpec((tile, HEADS * DIM), lambda i: (i, 0))
    one = pl.BlockSpec((tile, DIM), lambda i: (i, 0))
    piece = whole(32, 32, DIM)
    tile_rows = pl.BlockSpec((8, tile), lambda i: (0, i))
    rows_of = pl.BlockSpec((steps, 64, 2 * DIM), lambda i: (i, 0, 0))
    wide_heads = pl.BlockSpec((2 * tile, HEADS * DIM), lambda i: (i, 0))
    keep, send = pl.pallas_call(
        maps_kernel,
        grid=(2,),
        in_specs=[scalar, piece, wide_heads, wide_heads, pl.BlockSpec((8, 2 * tile), lambda i: (0, i))],
        out_specs=[rows_of, rows_of],
        out_shape=[sorted_rows] * 2,
        scratch_shapes=[parts, pltpu.VMEM((2 * tile, 2 * DIM), f32)],
        compiler_params=params(MAPS),
        name="maps",
    )(core, got, inputs, cotangent, rows)
    reduced = keep + near + lax.ppermute(send, "core", swap)
    reduced, got = lax.optimization_barrier((reduced, got))
    reduced = lax.all_to_all(reduced, "y", 0, 0)
    grad_inputs, grad_decay = pl.pallas_call(
        rest_kernel,
        grid=(steps,),
        in_specs=[
            piece, heads, heads, one, one, tile_rows, whole(8, TOK), heads,
            whole(BLOCKS, 8, TILE),
        ],
        out_specs=[heads, whole(HEADS, TOK)],
        out_shape=[shape(TOK, HEADS * DIM), shape(HEADS, TOK)],
        scratch_shapes=[parts, pltpu.VMEM((HEADS, 2 * DIM, DIM), bf16), pltpu.VMEM((steps, 8, tile), f32)],
        compiler_params=params(REST),
        name="rest",
    )(got, inputs, cotangent, in_map, out_map, rows, rows, gx, decay)
    reduced, grad_decay = lax.optimization_barrier((reduced, grad_decay))
    grad_in_map, grad_out_map = pl.pallas_call(
        sum_kernel, out_shape=[shape(64, DIM)] * 2, compiler_params=params(SCAN), name="sum"
    )(reduced)
    return (grad_inputs, grad_in_map, grad_out_map, grad_decay)


def solution(mesh):
    grid = Mesh(mesh.devices.reshape(4, 8, 8, 2), SEQ + HEAD)
    rows, columns = P(SEQ, None), P(SEQ, HEAD)
    return jax.shard_map(
        on_device,
        mesh=grid,
        in_specs=(columns, rows, rows, P(HEAD, SEQ), columns),
        out_specs=(columns, P(SEQ + HEAD, None), P(SEQ + HEAD, None), P(HEAD, SEQ)),
        check_vma=False,
    )
```

```python
import jax
import jax.numpy as jnp
from jax import lax
from jax.experimental import pallas as pl
from jax.experimental.pallas import tpu as pltpu
from jax.sharding import Mesh, PartitionSpec as P

f32, bf16 = jnp.float32, jnp.bfloat16
SEQ, HEAD = ("x", "z"), ("y", "core")
TOK, HEADS, DIM, TILE = 1024, 4, 128, 128
BLOCKS = TOK // TILE
STATES, LOCAL, SCAN, MAPS, REST = 56, 24, 4, 12, 56


def dot(a, b, dims):
    return lax.dot_general(a, b, (dims, ((), ())), preferred_element_type=f32)


def split(v):
    hi = v.astype(bf16)
    return hi, (v - hi.astype(f32)).astype(bf16)


def dot_wide(wide, exact):
    return dot(jnp.concatenate(split(wide), axis=1), jnp.concatenate([exact, exact], axis=0), ((1,), (0,)))


def running_sums(v, width, shift_suffix=True):
    lanes = v.shape[1]
    at = lax.broadcasted_iota(jnp.int32, v.shape, 1) & (width - 1)
    prefix = v
    suffix = jnp.where(at < width - 1, pltpu.roll(v, lanes - 1, 1), 0.0) if shift_suffix else v
    step = 1
    while step < width:
        prefix = prefix + jnp.where(at >= step, pltpu.roll(prefix, step, 1), 0.0)
        suffix = suffix + jnp.where(at < width - step, pltpu.roll(suffix, lanes - step, 1), 0.0)
        step *= 2
    return prefix, suffix


def state_kernel(x_ref, dy_ref, b_ref, c_ref, rate_ref, piece_ref, rows_ref, turned, total):
    step = pl.program_id(0)

    @pl.when(step == 0)
    def _():
        rates = jnp.concatenate([rate_ref[...], rate_ref[...]], axis=0)
        prefix, suffix = running_sums(rates, TOK)
        row = lax.broadcasted_iota(jnp.int32, rates.shape, 0)
        rows_ref[...] = jnp.exp(jnp.where(row < HEADS, suffix, prefix))
        totals = jnp.broadcast_to(jnp.exp(prefix[:, TOK - 1 :]), (8, DIM))
        total[0] = totals
        total[1] = jnp.concatenate([totals[2:], totals[:2]], axis=0)
        unit = lax.broadcasted_iota(jnp.int32, (DIM, DIM), 0) == lax.broadcasted_iota(jnp.int32, (DIM, DIM), 1)
        unit = unit.astype(f32).astype(bf16)
        turned[0] = dot(unit, b_ref[...], ((1,), (1,)))
        turned[1] = dot(unit, c_ref[...], ((1,), (1,)))

    for k in range(16):
        piece_ref[k, 0, 8] = total[step, 0:4, :]
    for h in range(2):
        for d, ref in enumerate((x_ref, dy_ref)):
            scaled = turned[d] * rows_ref[pl.ds(d * HEADS + 2 * step + h, 1), :]
            both = dot(jnp.concatenate(split(scaled), axis=0), ref[:, h * DIM : (h + 1) * DIM], ((1,), (0,)))
            state = both[:DIM] + both[DIM:]
            at = (d * 2 + h) * 2
            for k in range(16):
                piece_ref[k, 0, at] = state[8 * k : 8 * k + 4]
                piece_ref[k, 0, at + 1] = state[8 * k + 4 : 8 * k + 8]


def scan_kernel(got_ref, out_ref):
    for d in range(2):

        @pl.when(pl.program_id(0) == d)
        def _():
            for at in range(0, 16, 4):
                held = jnp.zeros((4, DIM), f32)
                for k in range(32) if d == 0 else reversed(range(32)):
                    out_ref[k, at : at + 4, :] = held
                    held = held * got_ref[k, 8, at // 8 : at // 8 + 1, :] + got_ref[k, d * 4 + at // 4]


def piece_of(got_ref, d, h):
    at = (d * 2 + h % 2) * 8
    return jnp.concatenate([got_ref[2 * k + h // 2, at : at + 8, :] for k in range(16)], axis=0)


def columns(rows):
    return jnp.concatenate([jnp.concatenate([rows[:, k : k + TILE]] * 16, axis=0).T for k in range(0, rows.shape[1], TILE)], axis=0)


def sort_rows(core_ref, rows_ref, keep_ref, send_ref):
    own = pl.multiple_of(core_ref[0] * 64, 64)
    for k in range(keep_ref.shape[0]):
        keep_ref[k] = rows_ref[pl.ds(k * 128 + own, 64), :]
        send_ref[k] = rows_ref[pl.ds(k * 128 + 64 - own, 64), :]


def block_sums(rate_ref, rb, sb, tb):
    rates = jnp.concatenate([rate_ref[...], rate_ref[...]], axis=0)
    prefix, suffix = running_sums(rates, TILE)
    for k in range(BLOCKS):
        rb[k] = prefix[:, k * TILE : (k + 1) * TILE]
        sb[k] = suffix[:, k * TILE : (k + 1) * TILE]
        if tb is not None:
            tb[k] = jnp.broadcast_to(jnp.exp(prefix[:, (k + 1) * TILE - 1 : (k + 1) * TILE]), (8, TILE))


def local_kernel(core_ref, x_ref, dy_ref, b_ref, c_ref, rate_ref, gx_ref, keep_ref, send_ref, decay_ref,
                 rb, sb, tb, part, held_ref, work_ref):
    block_sums(rate_ref, rb, sb, tb)
    causal = lax.broadcasted_iota(jnp.int32, (TILE, TILE), 0) <= lax.broadcasted_iota(jnp.int32, (TILE, TILE), 1)

    def block(j, nothing):
        at = pl.ds(pl.multiple_of(j * TILE, TILE), TILE)
        b, c, own = b_ref[at, :], c_ref[at, :], rb[j]
        scores = dot(b, c, ((1,), (1,)))
        scales = (jnp.exp(sb[j]), jnp.exp(own))
        turned = (b.astype(f32).T, c.astype(f32).T)
        joint = None
        for h in range(HEADS):
            lanes = slice(h * DIM, (h + 1) * DIM)
            x, dy = x_ref[at, lanes], dy_ref[at, lanes]
            across = jnp.broadcast_to(own[h : h + 1], (TILE, TILE))
            decay = jnp.where(causal, jnp.exp(across - across.T), 0.0)
            pairs = dot(x, dy, ((1,), (1,)))
            weights = decay * scores
            mine = decay * pairs
            joint = mine if joint is None else joint + mine
            product = weights * pairs
            gx_ref[at, lanes] = dot_wide(weights, dy)
            decay_ref[j, h : h + 1, :] = jnp.sum(product.T - product, axis=0, keepdims=True)
            for d, from_ in enumerate((x, dy)):
                wide = jnp.concatenate(split(turned[d] * scales[d][h : h + 1]), axis=0)
                both = dot(wide, from_, ((1,), (0,)))
                part[j, d * HEADS + h] = both[:DIM] + both[DIM:]
        work_ref[at, :DIM] = dot_wide(joint, c)
        work_ref[at, DIM : 2 * DIM] = dot_wide(joint.T, b)
        return nothing

    lax.fori_loop(0, BLOCKS, block, 0)
    for d in range(2):
        for h in range(HEADS):
            held = jnp.zeros((TILE, DIM), f32)
            for k in range(BLOCKS) if d == 0 else reversed(range(BLOCKS)):
                held_ref[k, d * HEADS + h] = jnp.concatenate(split(held), axis=1)
                held = held * tb[k, h : h + 1, :] + part[k, d * HEADS + h]
    def carried(j, nothing):
        at = pl.ds(pl.multiple_of(j * TILE, TILE), TILE)
        b, c = b_ref[at, :], c_ref[at, :]
        wide_b, wide_c = b.astype(f32), c.astype(f32)
        scale = jnp.concatenate([jnp.exp(sb[j, 0:HEADS, :]), jnp.exp(rb[j, 0:HEADS, :])], axis=0)
        cols = columns(scale)
        grad_in, grad_out = work_ref[at, :DIM], work_ref[at, DIM : 2 * DIM]
        for h in range(HEADS):
            lanes = slice(h * DIM, (h + 1) * DIM)
            after = held_ref[j, HEADS + h]
            to_end = jnp.broadcast_to(cols[:, h : h + 1], (TILE, DIM))
            stacked = jnp.concatenate([after[:, :DIM], after[:, DIM:]], axis=0)
            gx_ref[at, lanes] += to_end * dot(twice(b), stacked, ((1,), (0,)))
            fed_in = to_end * dot(twice(x_ref[at, lanes]), after, ((1,), (1,)))
            fed_out = cols[:, HEADS + h : HEADS + h + 1] * dot(twice(dy_ref[at, lanes]), held_ref[j, h], ((1,), (1,)))
            grad_in = grad_in + fed_in
            grad_out = grad_out + fed_out
            change = fed_in * wide_b - fed_out * wide_c
            decay_ref[j, h : h + 1, :] += jnp.sum(change.T, axis=0, keepdims=True)
        work_ref[at, :DIM] = grad_in
        work_ref[at, DIM : 2 * DIM] = grad_out
        return nothing

    lax.fori_loop(0, BLOCKS, carried, 0)
    sort_rows(core_ref, work_ref, keep_ref, send_ref)


def twice(v):
    return jnp.concatenate([v, v], axis=1)


def maps_kernel(core_ref, got_ref, x_ref, dy_ref, rows_ref, keep_ref, send_ref, parts, work):
    @pl.when(pl.program_id(0) == 0)
    def _():
        for d in range(2):
            for h in range(HEADS):
                parts[d * HEADS + h] = jnp.concatenate(split(piece_of(got_ref, d, h)), axis=1)

    cols = columns(rows_ref[...])
    for d, ref in ((1, x_ref), (0, dy_ref)):
        total = None
        for h in range(HEADS):
            at = (1 - d) * HEADS + h
            fed = dot(twice(ref[:, h * DIM : (h + 1) * DIM]), parts[d * HEADS + h], ((1,), (1,)))
            fed = cols[:, at : at + 1] * fed
            total = fed if total is None else total + fed
        work[:, (1 - d) * DIM : (2 - d) * DIM] = total
    sort_rows(core_ref, work, keep_ref, send_ref)


def rest_kernel(got_ref, x_ref, dy_ref, b_ref, c_ref, tile_rows_ref, rows_ref, gx0_ref, decay0_ref,
                gx_ref, decay_ref, parts, stacked, sums):
    step = pl.program_id(0)
    tile = x_ref.shape[0]

    @pl.when(step == 0)
    def _():
        for h in range(HEADS):
            for d in range(2):
                parts[d * HEADS + h] = jnp.concatenate(split(piece_of(got_ref, d, h)), axis=1)
            stacked[h] = jnp.concatenate(split(piece_of(got_ref, 1, h)), axis=0)

    b, c = b_ref[...], c_ref[...]
    wide_b, wide_c = b.astype(f32), c.astype(f32)
    cols = columns(tile_rows_ref[...])
    for h in range(HEADS):
        lanes = slice(h * DIM, (h + 1) * DIM)
        gx_ref[:, lanes] = gx0_ref[:, lanes] + cols[:, h : h + 1] * dot(twice(b), stacked[h], ((1,), (0,)))
        fed = dot(twice(x_ref[:, lanes]), parts[HEADS + h], ((1,), (1,))) * wide_b
        sums[step, h : h + 1, :] = jnp.sum(fed.T, axis=0, keepdims=True)
        fed = dot(twice(dy_ref[:, lanes]), parts[h], ((1,), (1,))) * wide_c
        sums[step, HEADS + h : HEADS + h + 1, :] = jnp.sum(fed.T, axis=0, keepdims=True)

    @pl.when(step == TOK // tile - 1)
    def _():
        rows = rows_ref[...]
        terms = jnp.concatenate([sums[k] for k in range(TOK // tile)], axis=1) * rows
        local = jnp.concatenate([decay0_ref[k, 0:HEADS, :] for k in range(BLOCKS)], axis=1)
        terms = terms + jnp.concatenate([local, jnp.zeros((HEADS, TOK), f32)], axis=0)
        at = lax.broadcasted_iota(jnp.int32, terms.shape, 1)
        moved = jnp.where(at >= 1, pltpu.roll(terms, 1, 1), 0.0)
        prefix, _ = running_sums(moved, TOK, False)
        _, suffix = running_sums(terms, TOK, False)
        decay = prefix[:HEADS] + suffix[HEADS:]
        which = lax.broadcasted_iota(jnp.int32, (HEADS, 1), 0)
        crossing = jnp.zeros((HEADS, 1), f32)
        for h in range(HEADS):
            both = jnp.sum(piece_of(got_ref, 0, h) * piece_of(got_ref, 1, h), axis=0, keepdims=True)
            both = jnp.sum(both, axis=1, keepdims=True)
            crossing = jnp.where(which == h, both, crossing)
        decay_ref[...] = decay + crossing * rows[HEADS:, TOK - 1 :]


def sum_kernel(parts_ref, in_ref, out_ref):
    total = parts_ref[0]
    for k in range(1, parts_ref.shape[0]):
        total = total + parts_ref[k]
    in_ref[...] = total[:, :DIM]
    out_ref[...] = total[:, DIM:]


def params(mib):
    return pltpu.CompilerParams(vmem_limit_bytes=mib << 20)


def shape(*dims, dtype=f32):
    return jax.ShapeDtypeStruct(dims, dtype)


def whole(*dims):
    return pl.BlockSpec(dims, lambda *_: (0,) * len(dims))


def on_device(inputs, in_map, out_map, log_decay, cotangent):
    half = pl.BlockSpec((TOK, 2 * DIM), lambda i: (0, i))
    pieces, rows = pl.pallas_call(
        state_kernel,
        grid=(2,),
        in_specs=[half, half, whole(TOK, DIM), whole(TOK, DIM), whole(HEADS, TOK)],
        out_specs=[pl.BlockSpec((16, 1, 9, 4, DIM), lambda i: (0, i, 0, 0, 0)), whole(8, TOK)],
        out_shape=[shape(16, 2, 9, 4, DIM), shape(8, TOK)],
        scratch_shapes=[pltpu.VMEM((2, DIM, TOK), f32), pltpu.VMEM((2, 8, DIM), f32)],
        compiler_params=params(STATES),
        name="states",
    )(inputs, cotangent, in_map, out_map, log_decay)
    got = lax.all_to_all(pieces.reshape(32, 9, 4, DIM), SEQ, 0, 0)
    sums = pltpu.VMEM((BLOCKS, 8, TILE), f32)
    core = lax.axis_index("core").astype(jnp.int32).reshape(1)
    scalar = pl.BlockSpec(memory_space=pltpu.SMEM)
    sorted_rows = shape(8, 64, 2 * DIM)
    gx, keep_near, send_near, decay = pl.pallas_call(
        local_kernel,
        in_specs=[scalar] + [whole(*v.shape) for v in (inputs, cotangent, in_map, out_map, log_decay)],
        out_shape=[shape(TOK, HEADS * DIM), sorted_rows, sorted_rows, shape(BLOCKS, 8, TILE)],
        scratch_shapes=[sums] * 3
        + [
            pltpu.VMEM((BLOCKS, 2 * HEADS, DIM, DIM), f32),
            pltpu.VMEM((BLOCKS, 2 * HEADS, DIM, 2 * DIM), bf16),
            pltpu.VMEM((TOK, 2 * DIM), f32),
        ],
        compiler_params=params(LOCAL),
        name="local",
    )(core, inputs, cotangent, in_map, out_map, log_decay)
    got, send_near = lax.optimization_barrier((got, send_near))
    scanned = pl.pallas_call(
        scan_kernel,
        grid=(2,),
        in_specs=[whole(32, 9, 4, DIM)],
        out_specs=pl.BlockSpec((32, 16, DIM), lambda i: (0, i, 0)),
        out_shape=pltpu.HBM((32, 32, DIM), f32),
        compiler_params=params(SCAN),
        name="scan",
    )(got)
    scanned, send_near = lax.optimization_barrier((scanned, send_near))
    got = lax.all_to_all(scanned, SEQ, 0, 0)
    swap = [(0, 1), (1, 0)]
    near = keep_near + lax.ppermute(send_near, "core", swap)
    got, near = lax.optimization_barrier((got, near))
    tile = 256
    steps = TOK // tile
    parts = pltpu.VMEM((2 * HEADS, DIM, 2 * DIM), bf16)
    heads = pl.BlockSpec((tile, HEADS * DIM), lambda i: (i, 0))
    one = pl.BlockSpec((tile, DIM), lambda i: (i, 0))
    piece = whole(32, 32, DIM)
    tile_rows = pl.BlockSpec((8, tile), lambda i: (0, i))
    rows_of = pl.BlockSpec((2 * steps, 64, 2 * DIM), lambda i: (i, 0, 0))
    wide_heads = pl.BlockSpec((4 * tile, HEADS * DIM), lambda i: (i, 0))
    keep, send = pl.pallas_call(
        maps_kernel,
        grid=(1,),
        in_specs=[scalar, piece, wide_heads, wide_heads, pl.BlockSpec((8, 4 * tile), lambda i: (0, i))],
        out_specs=[rows_of, rows_of],
        out_shape=[sorted_rows] * 2,
        scratch_shapes=[parts, pltpu.VMEM((4 * tile, 2 * DIM), f32)],
        compiler_params=params(MAPS),
        name="maps",
    )(core, got, inputs, cotangent, rows)
    reduced = keep + near + lax.ppermute(send, "core", swap)
    reduced, got = lax.optimization_barrier((reduced, got))
    reduced = lax.all_to_all(reduced, "y", 0, 0)
    grad_inputs, grad_decay = pl.pallas_call(
        rest_kernel,
        grid=(steps,),
        in_specs=[
            piece, heads, heads, one, one, tile_rows, whole(8, TOK), heads,
            whole(BLOCKS, 8, TILE),
        ],
        out_specs=[heads, whole(HEADS, TOK)],
        out_shape=[shape(TOK, HEADS * DIM), shape(HEADS, TOK)],
        scratch_shapes=[parts, pltpu.VMEM((HEADS, 2 * DIM, DIM), bf16), pltpu.VMEM((steps, 8, tile), f32)],
        compiler_params=params(REST),
        name="rest",
    )(got, inputs, cotangent, in_map, out_map, rows, rows, gx, decay)
    reduced, grad_decay = lax.optimization_barrier((reduced, grad_decay))
    grad_in_map, grad_out_map = pl.pallas_call(
        sum_kernel, out_shape=[shape(64, DIM)] * 2, compiler_params=params(SCAN), name="sum"
    )(reduced)
    return (grad_inputs, grad_in_map, grad_out_map, grad_decay)


def solution(mesh):
    grid = Mesh(mesh.devices.reshape(4, 8, 8, 2), SEQ + HEAD)
    rows, columns = P(SEQ, None), P(SEQ, HEAD)
    return jax.shard_map(
        on_device,
        mesh=grid,
        in_specs=(columns, rows, rows, P(HEAD, SEQ), columns),
        out_specs=(columns, P(SEQ + HEAD, None), P(SEQ + HEAD, None), P(HEAD, SEQ)),
        check_vma=False,
    )
```
